256 devices in a mesh: ctx: 64 (over x_lo, y, z), tp: 4 (over x_hi, core).
Axes of the slice: x: 4 (x_hi: 2, x_lo: 2; x = x_hi * 2 + x_lo), y: 4, z: 8, core: 2. Of those that a mesh axis runs over, the one named last changes fastest.
Arguments:
- stream_in: bfloat16 [65536, 4096], P('ctx', 'tp'), may hold values from -12 to 12
- features: bfloat16 [65536, 3, 4096], P('ctx', None, 'tp'), may hold values from -6 to 6
- mr_taps: float32 [3, 4096, 7], P(None, 'tp'), may hold values from -2 to 2
- mr_filter: bfloat16 [4096, 128], P('tp'), may hold values from -0.5 to 0.5
- norm_gain: float32 [4096], P('tp'), may hold values from 0.1 to 1.9
- li_taps: float32 [3, 4096, 7], P(None, 'tp'), may hold values from -2 to 2
- modal_rates: float32 [4096, 16], P('tp'), may hold values from 3.0517577e-07 to 0.1
- modal_weights: float32 [4096, 16], P('tp'), may hold values from -1.5 to 1.5
Outputs:
- mixed: bfloat16 [65536, 4096], P('ctx', 'tp')
The draws below stay inside these ranges and needn't reach their ends.
All inputs are finite; a program needn't handle non-finite values.
Results may differ from the reference program's by a relative error of at most 0.015.
Values may be sent and summed in bfloat16 or wider, within the bound.
No kernel may reach another device: no remote copies, remote signals or barrier semaphores. Data moves between devices by JAX's collectives and lax.ppermute only.
A program may use at most 256 MiB of HBM per device.

```python
import math
import jax
import jax.numpy as jnp
from jax import lax

D = 4096
MODES = 16
SEQ = 65536


def draw_stream_in(key, part):
    first_key, second_key = jax.random.split(key)
    channel_ramp = jnp.arange(D, dtype=jnp.float32) / D
    roughness = jax.random.uniform(second_key, (D,), jnp.float32, 0.7, 1.3)
    scales = jnp.sqrt(1.0 + 2.0 * channel_ramp) * roughness
    values_drawn = jnp.clip(jax.random.normal(first_key, (SEQ, D), jnp.float32), -5.0, 5.0)
    return (values_drawn * scales).astype(jnp.bfloat16)


def shard_levels(own_key, dims, shards, smallest, largest):
    level, own = 1.0, jax.random.fold_in(own_key, 6)
    for axis_at, parts in shards:
        draws = jnp.exp(jax.random.uniform(jax.random.fold_in(own, axis_at), (parts,), jnp.float32, smallest / len(shards), largest / len(shards)))
        level = level * jnp.repeat(draws, dims[axis_at] // parts).reshape([-1 if axis == axis_at else 1 for axis in range(len(dims))])
    return level


def normal_values(own_key, shape, deviation, most, cuts=(), held_as=jnp.bfloat16):
    factor_of = shard_levels(own_key, shape, cuts, -0.22, 0.18) if cuts else 1.0
    values = jax.random.normal(own_key, shape, jnp.float32) * deviation * factor_of
    return jnp.minimum(jnp.maximum(values, -most), most).astype(held_as)


def setup_inputs(seed: int = 0) -> dict:
    key_of = jax.random.split(jax.random.key(seed), 9)
    return {
        "stream_in": draw_stream_in(jax.random.fold_in(key_of[8], 71), 0),
        "features": normal_values(key_of[1], (SEQ, 3, D), 1.0, 6.0, ((0, 64), (2, 4))),
        "mr_taps": normal_values(key_of[2], (3, D, 7), 7 ** -0.5, 2.0, ((1, 4),), jnp.float32),
        "mr_filter": normal_values(key_of[3], (D, 128), 128 ** -0.5, 0.5, ((0, 4),)),
        "norm_gain": jnp.clip(1.0 + 0.18 * jax.random.normal(key_of[4], (D,), jnp.float32), 0.1, 1.9),
        "li_taps": normal_values(key_of[5], (3, D, 7), 7 ** -0.5, 2.0, ((1, 4),), jnp.float32),
        "modal_rates": jnp.clip(jnp.exp(math.log(0.1) - 12.699793 * jax.random.uniform(key_of[6], (D, MODES), jnp.float32) ** shard_levels(key_of[6], (D, MODES), ((0, 4),), -0.2, 0.2)), 3.0517577442878974e-07, 0.1),
        "modal_weights": normal_values(key_of[7], (D, MODES), MODES ** -0.5, 1.5, ((0, 4),), jnp.float32),
    }


epsilon = 1e-06
top_precision = lax.Precision.HIGHEST

def short_conv(rows_in, taps, row_count):
    summed = jnp.zeros((row_count, rows_in.shape[1]), jnp.float32)
    for tap_index in range(7):
        summed = summed + taps[:, tap_index] * rows_in[6 - tap_index:6 - tap_index + row_count].astype(jnp.float32)
    return summed

def featurize(rows_in, taps):
    padded = jnp.pad(rows_in, ((6, 0), (0, 0)))
    return short_conv(padded, taps, rows_in.shape[0])

def split_cols(matrix, width):
    return matrix.reshape(matrix.shape[0], -1, width).transpose(1, 0, 2)

def join_cols(pieces):
    return pieces.transpose(1, 0, 2).reshape(pieces.shape[1], -1)

def medium_group(operands):
    product_cols, filt_rows = operands
    group_width = product_cols.shape[1]
    block_count = SEQ // 64
    padded = jnp.pad(product_cols.astype(jnp.float32), ((128, 0), (0, 0))).reshape(block_count + 2, 64, group_width)
    lag_table = jnp.arange(64, dtype=jnp.int32)[:, None] + 128 - jnp.arange(192, dtype=jnp.int32)[None, :]
    valid = (lag_table >= 0) & (lag_table < 128)
    matrix = jnp.where(valid[None], filt_rows.astype(jnp.float32)[:, jnp.clip(lag_table, 0, 127)], 0.0)
    summed = jnp.zeros((block_count, 64, group_width), jnp.float32)
    for part_index in range(3):
        summed = summed + jnp.einsum('cij,bjc->bic', matrix[:, :, 64 * part_index:64 * part_index + 64], padded[part_index:part_index + block_count], precision=top_precision)
    return summed.reshape(SEQ, group_width)

def long_group(operands):
    product_cols, rates, weights = operands
    group_width = product_cols.shape[1]
    block_count = SEQ // 64
    block_groups = product_cols.astype(jnp.float32).reshape(block_count, 64, group_width)
    scaled = weights * jnp.sqrt(1.0 - jnp.exp(-2.0 * rates))
    lags = jnp.arange(64, dtype=jnp.float32)
    near_taps = lax.optimization_barrier(jnp.sum(scaled[:, None, :] * jnp.exp(-rates[:, None, :] * lags[None, :, None]), axis=2))
    lag_table = jnp.arange(64, dtype=jnp.int32)[:, None] - jnp.arange(64, dtype=jnp.int32)[None, :]
    matrix = jnp.where((lag_table >= 0)[None], near_taps[:, jnp.clip(lag_table, 0, 63)], 0.0)
    near = jnp.einsum('cij,bjc->bic', matrix, block_groups, precision=top_precision)
    outgoing_state = jnp.exp(-rates[None] * (63.0 - lags)[:, None, None])
    produced_output = jnp.einsum('bjc,jcn->bcn', block_groups, outgoing_state, precision=top_precision)
    decay = jnp.exp(-rates * 64.0)

    def advance(state, emit):
        return (state * decay + emit, state)
    unused, states = lax.scan(advance, jnp.zeros_like(decay), produced_output)
    incoming_state = scaled[None] * jnp.exp(-rates[None] * (lags + 1.0)[:, None, None])
    distant_taps = jnp.einsum('bcn,icn->bic', states, incoming_state, precision=top_precision)
    return (near + distant_taps).reshape(SEQ, group_width)

def reference(stream_in, features, mr_taps, mr_filter, norm_gain, li_taps, modal_rates, modal_weights):
    group_width = min(256, D)
    gate_one = featurize(features[:, 0], mr_taps[0])
    keys_one = featurize(features[:, 1], mr_taps[1])
    vals_one = featurize(features[:, 2], mr_taps[2])
    product_one = (keys_one * vals_one).astype(jnp.bfloat16)
    medium = join_cols(lax.map(medium_group, (split_cols(product_one, group_width), mr_filter.reshape(-1, group_width, 128))))
    stream = stream_in.astype(jnp.float32) + gate_one * medium
    squares = lax.optimization_barrier(jnp.sum(stream * stream, axis=1)) / D
    normed = (stream * lax.rsqrt(squares + epsilon)[:, None] * norm_gain).astype(jnp.bfloat16)
    gate_two = featurize(normed, li_taps[0])
    keys_two = featurize(normed, li_taps[1])
    vals_two = featurize(normed, li_taps[2])
    product_two = (keys_two * vals_two).astype(jnp.bfloat16)
    long_out = join_cols(lax.map(long_group, (split_cols(product_two, group_width), modal_rates.reshape(-1, group_width, MODES), modal_weights.reshape(-1, group_width, MODES))))
    return (stream + gate_two * long_out).astype(jnp.bfloat16)
```

```python
import functools

import jax
import jax.numpy as jnp
import numpy as np
from jax import lax
from jax.experimental import pallas as pl
from jax.experimental.pallas import tpu as pltpu
from jax.sharding import PartitionSpec as P

D = 4096
EPS = 1e-06
MODES = 16
B = 128
HIGH = lax.Precision.HIGHEST
F32 = jnp.float32
BF16 = jnp.bfloat16
VMEM_LIMIT = 40 * 2**20


def dft_tables():
    j = np.arange(2 * B)
    k = np.arange(B)
    angle = np.pi * (2 * k[:, None] + 1) * j[None, :] / (2 * B)
    cos, sin = np.cos(angle), np.sin(angle)
    forward = np.concatenate([cos, -sin], axis=0)
    inverse = np.concatenate([cos.T, -sin.T], axis=1) / B
    return forward, inverse


def params():
    return pltpu.CompilerParams(vmem_limit_bytes=VMEM_LIMIT)


def cost(flops, bytes_accessed):
    return pl.CostEstimate(flops=flops, bytes_accessed=bytes_accessed, transcendentals=0)


def conv7(rows_ref, taps, start, count):
    total = taps[0:1] * rows_ref[pl.ds(start, count), :]
    for tap in range(1, 7):
        total = total + taps[tap : tap + 1] * rows_ref[pl.ds(start - tap, count), :]
    return total


def tail_kernel(feat_ref, stream_ref, taps_ref, filt_ref, out_ref, feat, prod):
    n_in, n_prod = 160, 144
    first = 256 - n_in
    for s in range(3):
        feat[s] = feat_ref[s, first:256, :].astype(F32)
    keys = conv7(feat.at[1], taps_ref[1], 16, n_prod)
    vals = conv7(feat.at[2], taps_ref[2], 16, n_prod)
    product = (keys * vals).astype(BF16)
    prod[...] = product.astype(F32)
    medium = jnp.zeros((8, 128), F32)
    for lag in range(128):
        medium = medium + filt_ref[lag : lag + 1, :] * prod[pl.ds(136 - lag, 8), :]
    gate = conv7(feat.at[0], taps_ref[0], n_in - 8, 8)
    stream = stream_ref[248:256, :].astype(F32) + gate * medium
    high = stream.astype(BF16)
    out_ref[0:128, :] = product[16:144]
    for s in range(3):
        out_ref[128 + 8 * s : 136 + 8 * s, :] = feat_ref[s, 248:256, :]
    out_ref[152:160, :] = high
    out_ref[160:168, :] = (stream - high.astype(F32)).astype(BF16)


def mr_tail(feat, stream_in, taps, filt):
    rows, chans = stream_in.shape
    last = rows // 256 - 1
    return pl.pallas_call(
        tail_kernel,
        grid=(chans // 128,),
        in_specs=[
            pl.BlockSpec((3, 256, 128), lambda c: (0, last, c)),
            pl.BlockSpec((256, 128), lambda c: (last, c)),
            pl.BlockSpec((3, 7, 128), lambda c: (0, 0, c)),
            pl.BlockSpec((128, 128), lambda c: (0, c)),
        ],
        out_specs=pl.BlockSpec((168, 128), lambda c: (0, c)),
        out_shape=jax.ShapeDtypeStruct((168, chans), BF16),
        scratch_shapes=[pltpu.VMEM((3, 160, 128), F32), pltpu.VMEM((144, 128), F32)],
        compiler_params=params(),
        cost_estimate=cost(20 * 10**6, 2 * 10**6),
        name="mr_tail",
    )(feat, stream_in, taps, filt)


def spectral(window, forward, real, imag, inverse):
    spec = jnp.dot(forward, window, preferred_element_type=F32)
    xr, xi = spec[:B], spec[B:]
    out = jnp.concatenate([xr * real - xi * imag, xr * imag + xi * real], axis=0)
    return jnp.dot(inverse, out.astype(BF16), preferred_element_type=F32)


def put_row_sums(squares, count):
    ones = jnp.ones((8, 128), F32)
    return lax.dot_general(
        ones, squares, (((1,), (1,)), ((), ())), precision=HIGH, preferred_element_type=F32
    )


def mr_rows(feat_ref, stream_ref, taps_ref, spec_ref, fwd_ref, inv_ref, out_ref, feat, prod, sums,
            first, blocks):
    forward, inverse = fwd_ref[...], inv_ref[...]
    for half in range(2):
        lanes = slice(128 * half, 128 * half + 128)
        for b in range(blocks + 1):
            if first == 0 and b == 0:
                continue
            start = 8 + (b - 1) * B if first == 0 else 8 + b * B
            keys = conv7(feat.at[1, half], taps_ref[1, :, lanes], start, B)
            vals = conv7(feat.at[2, half], taps_ref[2, :, lanes], start, B)
            prod[b * B : (b + 1) * B, lanes] = (keys * vals).astype(BF16)
    for b in range(blocks):
        medium = spectral(prod[b * B : (b + 2) * B, :], forward, spec_ref[0], spec_ref[1], inverse)
        for half in range(2):
            lanes = slice(128 * half, 128 * half + 128)
            start = 8 + b * B if first == 0 else 8 + (b + 1) * B
            gate = conv7(feat.at[0, half], taps_ref[0, :, lanes], start, B)
            rows = slice(b * B, (b + 1) * B)
            stream = stream_ref[first + b * B : first + (b + 1) * B, lanes].astype(F32)
            stream = stream + gate * medium[:, lanes]
            out_ref[rows, lanes] = stream
            sums[rows, :] += stream * stream


def upper_kernel(feat_ref, stream_ref, taps_ref, spec_ref, fwd_ref, inv_ref, out_ref, sum_ref,
                 feat, prod, sums, *, blocks):
    step = pl.program_id(0)

    @pl.when(step == 0)
    def _():
        sums[...] = jnp.zeros_like(sums)

    for s in range(3):
        for half in range(2):
            feat[s, half] = feat_ref[s, 120:, 128 * half : 128 * half + 128].astype(F32)
    mr_rows(feat_ref, stream_ref, taps_ref, spec_ref, fwd_ref, inv_ref, out_ref, feat, prod, sums,
            2 * B, blocks)

    @pl.when(step == pl.num_programs(0) - 1)
    def _():
        for b in range(blocks):
            sum_ref[b] = put_row_sums(sums[b * B : (b + 1) * B, :], B)


def mr_upper(feat, stream_in, taps, spec, forward, inverse):
    rows, chans = stream_in.shape
    blocks = rows // B - 2
    return pl.pallas_call(
        functools.partial(upper_kernel, blocks=blocks),
        grid=(chans // 256,),
        in_specs=[
            pl.BlockSpec((3, rows, 256), lambda c: (0, 0, c)),
            pl.BlockSpec((rows, 256), lambda c: (0, c)),
            pl.BlockSpec((3, 7, 256), lambda c: (0, 0, c)),
            pl.BlockSpec((2, B, 256), lambda c: (0, 0, c)),
            pl.BlockSpec((2 * B, 2 * B), lambda c: (0, 0)),
            pl.BlockSpec((B, 2 * B), lambda c: (0, 0)),
        ],
        out_specs=[
            pl.BlockSpec((blocks * B, 256), lambda c: (0, c)),
            pl.BlockSpec((blocks, 8, 128), lambda c: (0, 0, 0)),
        ],
        out_shape=[
            jax.ShapeDtypeStruct((blocks * B, chans), F32),
            jax.ShapeDtypeStruct((blocks, 8, 128), F32),
        ],
        scratch_shapes=[
            pltpu.VMEM((3, 2, rows - 120, 128), F32),
            pltpu.VMEM(((blocks + 1) * B, 256), BF16),
            pltpu.VMEM((blocks * B, 128), F32),
        ],
        compiler_params=params(),
        cost_estimate=cost(2 * 10**9, 14 * 10**6),
        name="mr_upper",
    )(feat, stream_in, taps, spec, forward, inverse)


def lower_kernel(feat_ref, stream_ref, taps_ref, spec_ref, fwd_ref, inv_ref, halo_ref, upper_ref,
                 out_ref, sum_ref, feat, prod, sums, *, blocks):
    step = pl.program_id(0)

    @pl.when(step == 0)
    def _():
        sums[...] = jnp.zeros_like(sums)

    for half in range(2):
        lanes = slice(128 * half, 128 * half + 128)
        for s in range(3):
            feat[s, half, 0:8] = halo_ref[128 + 8 * s : 136 + 8 * s, lanes].astype(F32)
            feat[s, half, 8:] = feat_ref[s, :, lanes].astype(F32)
        before = halo_ref[152:160, lanes].astype(F32) + halo_ref[160:168, lanes].astype(F32)
        sums[2 * B : 2 * B + 8, :] += before * before
    prod[0:B, :] = halo_ref[0:B, :]
    mr_rows(feat_ref, stream_ref, taps_ref, spec_ref, fwd_ref, inv_ref, out_ref, feat, prod, sums,
            0, 2)

    @pl.when(step == pl.num_programs(0) - 1)
    def _():
        for b in range(3):
            sum_ref[b] = put_row_sums(sums[b * B : (b + 1) * B, :], B)
        sum_ref[3:] = upper_ref[...]


def mr_lower(feat, stream_in, taps, spec, forward, inverse, halo, upper):
    rows, chans = stream_in.shape
    blocks = upper.shape[0]
    return pl.pallas_call(
        functools.partial(lower_kernel, blocks=blocks),
        grid=(chans // 256,),
        in_specs=[
            pl.BlockSpec((3, 2 * B, 256), lambda c: (0, 0, c)),
            pl.BlockSpec((2 * B, 256), lambda c: (0, c)),
            pl.BlockSpec((3, 7, 256), lambda c: (0, 0, c)),
            pl.BlockSpec((2, B, 256), lambda c: (0, 0, c)),
            pl.BlockSpec((2 * B, 2 * B), lambda c: (0, 0)),
            pl.BlockSpec((B, 2 * B), lambda c: (0, 0)),
            pl.BlockSpec((168, 256), lambda c: (0, c)),
            pl.BlockSpec((blocks, 8, 128), lambda c: (0, 0, 0)),
        ],
        out_specs=[
            pl.BlockSpec((2 * B, 256), lambda c: (0, c)),
            pl.BlockSpec((blocks + 3, 8, 128), lambda c: (0, 0, 0)),
        ],
        out_shape=[
            jax.ShapeDtypeStruct((2 * B, chans), F32),
            jax.ShapeDtypeStruct((blocks + 3, 8, 128), F32),
        ],
        scratch_shapes=[
            pltpu.VMEM((3, 2, 2 * B + 8, 128), F32),
            pltpu.VMEM((3 * B, 256), BF16),
            pltpu.VMEM((3 * B, 128), F32),
        ],
        compiler_params=params(),
        cost_estimate=cost(7 * 10**8, 4 * 10**6),
        name="mr_lower",
    )(feat, stream_in, taps, spec, forward, inverse, halo, upper)


def state_kernel(low_ref, up_ref, halo_ref, s0_ref, s1_ref, s2_ref, s3_ref, gain_ref, taps_ref,
                 q8_ref, qs_ref, normed_ref, prod_ref, state_ref, inv, rows_f32, *, blocks):
    step = pl.program_id(0)

    @pl.when(step == 0)
    def _():
        total = s0_ref[...] + s1_ref[...] + s2_ref[...] + s3_ref[...]
        scale = lax.rsqrt(total * (1.0 / D) + EPS)
        for b in range(blocks + 1):
            spread = jnp.broadcast_to(scale[b, 0:1, :], (B, B))
            inv[b * B : (b + 1) * B, :] = jnp.transpose(spread)

    gain = gain_ref[...]
    before = halo_ref[0:8, :].astype(F32) + halo_ref[8:16, :].astype(F32)
    before = (before * inv[2 * B : 2 * B + 8, :] * gain).astype(BF16)
    normed_ref[0:8, :] = before
    rows_f32[0:8, :] = before.astype(F32)
    acc = [jnp.zeros((8, 128), F32) for _ in range(MODES)]
    q8 = [jnp.broadcast_to(q8_ref[n : n + 1, :], (8, 128)) for n in range(MODES)]
    for b in range(blocks):
        if b < 2:
            x = low_ref[b * B : (b + 1) * B, :]
            scale = inv[b * B : (b + 1) * B, :]
        else:
            x = up_ref[(b - 2) * B : (b - 1) * B, :]
            scale = inv[(b + 1) * B : (b + 2) * B, :]
        normed = (x * scale * gain).astype(BF16)
        start = 8 + b * B
        normed_ref[start : start + B, :] = normed
        rows_f32[start : start + B, :] = normed.astype(F32)
        keys = conv7(rows_f32, taps_ref[1], start, B)
        vals = conv7(rows_f32, taps_ref[2], start, B)
        product = (keys * vals).astype(BF16)
        prod_ref[b * B : (b + 1) * B, :] = product
        wide = product.astype(F32)
        for i in range(B // 8):
            part = wide[8 * i : 8 * i + 8]
            acc = [a * q + part for a, q in zip(acc, q8)]
        for n in range(MODES):
            state_ref[b, n : n + 1, :] = jnp.sum(acc[n] * qs_ref[n], axis=0, keepdims=True)


def li_states(low, up, halo, sums, gain, taps, q8, qs):
    chans = low.shape[1]
    rows = low.shape[0] + up.shape[0]
    blocks = rows // B
    sum_spec = pl.BlockSpec(sums[0].shape, lambda c: (0, 0, 0))
    return pl.pallas_call(
        functools.partial(state_kernel, blocks=blocks),
        grid=(chans // 128,),
        in_specs=[
            pl.BlockSpec((2 * B, 128), lambda c: (0, c)),
            pl.BlockSpec((rows - 2 * B, 128), lambda c: (0, c)),
            pl.BlockSpec((16, 128), lambda c: (0, c)),
            sum_spec, sum_spec, sum_spec, sum_spec,
            pl.BlockSpec((1, 128), lambda c: (0, c)),
            pl.BlockSpec((3, 7, 128), lambda c: (0, 0, c)),
            pl.BlockSpec((MODES, 128), lambda c: (0, c)),
            pl.BlockSpec((MODES, 8, 128), lambda c: (0, 0, c)),
        ],
        out_specs=[
            pl.BlockSpec((8 + rows, 128), lambda c: (0, c)),
            pl.BlockSpec((rows, 128), lambda c: (0, c)),
            pl.BlockSpec((blocks, MODES, 128), lambda c: (0, 0, c)),
        ],
        out_shape=[
            jax.ShapeDtypeStruct((8 + rows, chans), BF16),
            jax.ShapeDtypeStruct((rows, chans), BF16),
            jax.ShapeDtypeStruct((blocks, MODES, chans), F32),
        ],
        scratch_shapes=[
            pltpu.VMEM(((blocks + 1) * B, 128), F32),
            pltpu.VMEM((8 + rows, 128), F32),
        ],
        compiler_params=params(),
        cost_estimate=cost(90 * 10**6, 9 * 10**6),
        name="li_states",
    )(low, up, halo, *sums, gain, taps, q8, qs)


def near_kernel(low_ref, up_ref, normed_ref, prod_ref, taps_ref, spec_ref, fwd_ref, inv_ref,
                base_ref, gate_ref, rows_f32, *, blocks):
    forward, inverse = fwd_ref[...], inv_ref[...]
    for half in range(2):
        rows_f32[half] = normed_ref[:, 128 * half : 128 * half + 128].astype(F32)
    for b in range(blocks):
        rows = slice(b * B, (b + 1) * B)
        near = spectral(prod_ref[rows, :], forward, spec_ref[0], spec_ref[1], inverse)
        for half in range(2):
            lanes = slice(128 * half, 128 * half + 128)
            gate = conv7(rows_f32.at[half], taps_ref[0, :, lanes], 8 + b * B, B)
            stream = low_ref[rows, lanes] if b < 2 else up_ref[(b - 2) * B : (b - 1) * B, lanes]
            base_ref[rows, lanes] = stream + gate * near[:, lanes]
            gate_ref[rows, lanes] = gate


def li_near(low, up, normed, product, taps, spec, forward, inverse):
    rows, chans = product.shape
    return pl.pallas_call(
        functools.partial(near_kernel, blocks=rows // B),
        grid=(chans // 256,),
        in_specs=[
            pl.BlockSpec((2 * B, 256), lambda c: (0, c)),
            pl.BlockSpec((rows - 2 * B, 256), lambda c: (0, c)),
            pl.BlockSpec((8 + rows, 256), lambda c: (0, c)),
            pl.BlockSpec((rows, 256), lambda c: (0, c)),
            pl.BlockSpec((3, 7, 256), lambda c: (0, 0, c)),
            pl.BlockSpec((2, B, 256), lambda c: (0, 0, c)),
            pl.BlockSpec((2 * B, B), lambda c: (0, 0)),
            pl.BlockSpec((B, 2 * B), lambda c: (0, 0)),
        ],
        out_specs=[
            pl.BlockSpec((rows, 256), lambda c: (0, c)),
            pl.BlockSpec((rows, 256), lambda c: (0, c)),
        ],
        out_shape=[jax.ShapeDtypeStruct((rows, chans), F32)] * 2,
        scratch_shapes=[pltpu.VMEM((2, 8 + rows, 128), F32)],
        compiler_params=params(),
        cost_estimate=cost(10**9, 16 * 10**6),
        name="li_near",
    )(low, up, normed, product, taps, spec, forward, inverse)


def far_kernel(base_ref, gate_ref, state_ref, in_ref, q8_ref, q128_ref, wq_ref, out_ref, *, blocks):
    q8 = [jnp.broadcast_to(q8_ref[n : n + 1, :], (8, 128)) for n in range(MODES)]
    incoming = in_ref[...]
    for b in range(blocks):
        here = incoming if b == 0 else incoming + state_ref[b - 1]
        incoming = incoming * q128_ref[...]
        modes = [wq_ref[n] * here[n : n + 1, :] for n in range(MODES)]
        for i in range(B // 8):
            level = modes
            while len(level) > 1:
                level = [a + c for a, c in zip(level[::2], level[1::2])]
            rows = slice(b * B + 8 * i, b * B + 8 * i + 8)
            out_ref[rows, :] = (base_ref[rows, :] + gate_ref[rows, :] * level[0]).astype(BF16)
            if i < B // 8 - 1:
                modes = [m * q for m, q in zip(modes, q8)]


def li_far(base, gate, states, incoming, q8, q128, wq):
    rows, chans = base.shape
    blocks = rows // B
    return pl.pallas_call(
        functools.partial(far_kernel, blocks=blocks),
        grid=(chans // 128,),
        in_specs=[
            pl.BlockSpec((rows, 128), lambda c: (0, c)),
            pl.BlockSpec((rows, 128), lambda c: (0, c)),
            pl.BlockSpec((blocks, MODES, 128), lambda c: (0, 0, c)),
            pl.BlockSpec((MODES, 128), lambda c: (0, c)),
            pl.BlockSpec((MODES, 128), lambda c: (0, c)),
            pl.BlockSpec((MODES, 128), lambda c: (0, c)),
            pl.BlockSpec((MODES, 8, 128), lambda c: (0, 0, c)),
        ],
        out_specs=pl.BlockSpec((rows, 128), lambda c: (0, c)),
        out_shape=jax.ShapeDtypeStruct((rows, chans), BF16),
        compiler_params=params(),
        cost_estimate=cost(70 * 10**6, 10 * 10**6),
        name="li_far",
    )(base, gate, states, incoming, q8, q128, wq)


def ahead(value, steps):
    count = lax.axis_size("ctx")
    if steps >= count:
        return None
    return lax.ppermute(value, "ctx", [(i, i + steps) for i in range(count - steps)])


def incoming_states(outgoing, rates, rows):
    def gathered(value, offsets, unit, own):
        total = value if own else None
        for k in offsets:
            moved = ahead(value, k * unit)
            if moved is None:
                continue
            power = (k if own else k - 1) * unit
            term = moved * jnp.exp(-rates * float(rows * power)) if power else moved
            total = term if total is None else total + term
        return total

    with jax.named_scope("scan_states"):
        value = gathered(outgoing, (1, 2, 3, 4), 1, False)
        unit = 4
        while unit < lax.axis_size("ctx"):
            value = gathered(value, (1, 2, 3), unit, True)
            unit *= 4
    return value


def body(stream_in, features, mr_taps, mr_filter, norm_gain, li_taps, modal_rates, modal_weights):
    rows = stream_in.shape[0]
    feat = jnp.transpose(features, (1, 0, 2))
    mr_t = jnp.transpose(mr_taps, (0, 2, 1))
    li_t = jnp.transpose(li_taps, (0, 2, 1))
    rates = jnp.transpose(modal_rates)
    weights = jnp.transpose(modal_weights)
    gain = norm_gain[None, :]
    fwd_np, inv_np = dft_tables()
    forward = jnp.asarray(fwd_np, BF16)
    inverse = jnp.asarray(inv_np, BF16)
    half_fwd = jnp.asarray(fwd_np[:, :B], F32)

    filt = jnp.transpose(mr_filter).astype(F32)
    bundle = mr_tail(feat, stream_in, mr_t, filt)
    halo = ahead(bundle, 1)

    mr_spec = jnp.dot(half_fwd, filt, precision=HIGH).reshape(2, B, -1)
    scaled = weights * jnp.sqrt(1.0 - jnp.exp(-2.0 * rates))
    lags = jnp.arange(B, dtype=F32)
    near_taps = jnp.sum(scaled[None] * jnp.exp(-rates[None] * lags[:, None, None]), axis=1)
    li_spec = jnp.dot(half_fwd, near_taps, precision=HIGH).reshape(2, B, -1)
    within = jnp.arange(8, dtype=F32)[None, :, None]
    q8 = jnp.exp(-8.0 * rates)
    q128 = jnp.exp(-float(B) * rates)
    qs = jnp.exp(-rates[:, None, :] * (7.0 - within))
    wq = scaled[:, None, :] * jnp.exp(-rates[:, None, :] * (within + 1.0))

    up, up_sums = mr_upper(feat, stream_in, mr_t, mr_spec, forward, inverse[B:])
    low, own = mr_lower(feat, stream_in, mr_t, mr_spec, forward, inverse[B:], halo, up_sums)
    ways = lax.axis_size("tp")
    sums = [own] + [
        lax.ppermute(own, "tp", [(i, (i + k) % ways) for i in range(ways)]) for k in range(1, ways)
    ]
    normed, product, states = li_states(low, up, halo[152:168], sums, gain, li_t, q8, qs)
    incoming = incoming_states(states[-1], rates, rows)
    base, gate = li_near(low, up, normed, product, li_t, li_spec, forward[:, :B], inverse[:B])
    return li_far(base, gate, states, incoming, q8, q128, wq)


def solution(mesh):
    in_specs = (
        P("ctx", "tp"),
        P("ctx", None, "tp"),
        P(None, "tp", None),
        P("tp", None),
        P("tp"),
        P(None, "tp", None),
        P("tp", None),
        P("tp", None),
    )
    return jax.shard_map(
        body, mesh=mesh, in_specs=in_specs, out_specs=P("ctx", "tp"), check_vma=False
    )
```

```python
import functools

import jax
import jax.numpy as jnp
import numpy as np
from jax import lax
from jax.experimental import pallas as pl
from jax.experimental.pallas import tpu as pltpu
from jax.sharding import PartitionSpec as P

D = 4096
EPS = 1e-06
MODES = 16
B = 128
HIGH = lax.Precision.HIGHEST
F32 = jnp.float32
BF16 = jnp.bfloat16


def dft_tables():
    j = np.arange(2 * B)
    k = np.arange(B)
    angle = np.pi * (2 * k[:, None] + 1) * j[None, :] / (2 * B)
    cos, sin = np.cos(angle), np.sin(angle)
    forward = np.concatenate([cos, -sin], axis=0)
    inverse = np.concatenate([cos.T, -sin.T], axis=1) / B
    return forward, inverse


def params(mib):
    return pltpu.CompilerParams(vmem_limit_bytes=mib * 2**20)


def in_hbm(*values):
    return [pltpu.with_memory_space_constraint(value, pltpu.HBM) for value in values]


def cost(flops, bytes_accessed):
    return pl.CostEstimate(flops=flops, bytes_accessed=bytes_accessed, transcendentals=0)


def conv7(rows_ref, taps, start, count):
    total = taps[0:1] * rows_ref[pl.ds(start, count), :]
    for tap in range(1, 7):
        total = total + taps[tap : tap + 1] * rows_ref[pl.ds(start - tap, count), :]
    return total


def tail_kernel(feat_ref, stream_ref, taps_ref, filt_ref, fwd_ref, out_ref, spec_ref, feat, prod, filt):
    n_in, n_prod = 160, 144
    first = 256 - n_in
    turned = jnp.transpose(filt_ref[...].astype(F32))
    filt[...] = turned
    twice = jnp.concatenate([turned, turned], axis=0).astype(BF16)
    spec = jnp.dot(fwd_ref[...], twice, preferred_element_type=F32)
    spec_ref[0] = spec[:B]
    spec_ref[1] = spec[B:]
    for half in range(2):
        lanes = slice(128 * half, 128 * half + 128)
        for s in range(3):
            feat[s] = feat_ref[s, first:256, lanes].astype(F32)
        keys = conv7(feat.at[1], taps_ref[1, :, lanes], 16, n_prod)
        vals = conv7(feat.at[2], taps_ref[2, :, lanes], 16, n_prod)
        product = (keys * vals).astype(BF16)
        prod[...] = product.astype(F32)
        medium = jnp.zeros((8, 128), F32)
        for lag in range(128):
            medium = medium + filt[lag : lag + 1, lanes] * prod[pl.ds(136 - lag, 8), :]
        gate = conv7(feat.at[0], taps_ref[0, :, lanes], n_in - 8, 8)
        stream = stream_ref[8:16, lanes].astype(F32) + gate * medium
        high = stream.astype(BF16)
        out_ref[0:128, lanes] = product[16:144]
        for s in range(3):
            out_ref[128 + 8 * s : 136 + 8 * s, lanes] = feat_ref[s, 248:256, lanes]
        out_ref[152:160, lanes] = high
        out_ref[160:168, lanes] = (stream - high.astype(F32)).astype(BF16)


def mr_tail(feat, stream_in, taps, filt, forward):
    rows, chans = stream_in.shape
    last = rows // 256 - 1
    end = rows // 16 - 1
    return pl.pallas_call(
        tail_kernel,
        grid=(chans // 256,),
        in_specs=[
            pl.BlockSpec((3, 256, 256), lambda c: (0, last, c)),
            pl.BlockSpec((16, 256), lambda c: (end, c)),
            pl.BlockSpec((3, 7, 256), lambda c: (0, 0, c)),
            pl.BlockSpec((256, 128), lambda c: (c, 0)),
            pl.BlockSpec((2 * B, 2 * B), lambda c: (0, 0)),
        ],
        out_specs=[
            pl.BlockSpec((168, 256), lambda c: (0, c)),
            pl.BlockSpec((2, B, 256), lambda c: (0, 0, c)),
        ],
        out_shape=[
            jax.ShapeDtypeStruct((168, chans), BF16),
            jax.ShapeDtypeStruct((2, B, chans), F32),
        ],
        scratch_shapes=[
            pltpu.VMEM((3, 160, 128), F32),
            pltpu.VMEM((144, 128), F32),
            pltpu.VMEM((128, 256), F32),
        ],
        compiler_params=params(12),
        cost_estimate=cost(20 * 10**6, 2 * 10**6),
        name="mr_tail",
    )(feat, stream_in, *in_hbm(taps, filt, forward))


def spectral(window, forward, real, imag, inverse):
    spec = jnp.dot(forward, window, preferred_element_type=F32)
    xr, xi = spec[:B], spec[B:]
    out = jnp.concatenate([xr * real - xi * imag, xr * imag + xi * real], axis=0)
    return jnp.dot(inverse, out.astype(BF16), preferred_element_type=F32)


def put_row_sums(squares, count):
    ones = jnp.ones((8, 128), F32)
    return lax.dot_general(
        ones, squares, (((1,), (1,)), ((), ())), precision=HIGH, preferred_element_type=F32
    )


def mr_rows(feat_ref, stream_ref, taps_ref, spec_ref, fwd_ref, inv_ref, out_ref, feat, prod, sums,
            first, blocks):
    forward, inverse = fwd_ref[...], inv_ref[...]
    for half in range(2):
        lanes = slice(128 * half, 128 * half + 128)
        for b in range(blocks + 1):
            if first == 0 and b == 0:
                continue
            start = 8 + (b - 1) * B if first == 0 else 8 + b * B
            keys = conv7(feat.at[1, half], taps_ref[1, :, lanes], start, B)
            vals = conv7(feat.at[2, half], taps_ref[2, :, lanes], start, B)
            prod[b * B : (b + 1) * B, lanes] = (keys * vals).astype(BF16)
    for b in range(blocks):
        medium = spectral(prod[b * B : (b + 2) * B, :], forward, spec_ref[0], spec_ref[1], inverse)
        for half in range(2):
            lanes = slice(128 * half, 128 * half + 128)
            start = 8 + b * B if first == 0 else 8 + (b + 1) * B
            gate = conv7(feat.at[0, half], taps_ref[0, :, lanes], start, B)
            rows = slice(b * B, (b + 1) * B)
            stream = stream_ref[first + b * B : first + (b + 1) * B, lanes].astype(F32)
            stream = stream + gate * medium[:, lanes]
            out_ref[rows, lanes] = stream
            sums[rows, :] += stream * stream


def upper_kernel(feat_ref, stream_ref, taps_ref, spec_ref, fwd_ref, inv_ref, out_ref, sum_ref,
                 feat, prod, sums, *, blocks):
    step = pl.program_id(0)

    @pl.when(step == 0)
    def _():
        sums[...] = jnp.zeros_like(sums)

    for s in range(3):
        for half in range(2):
            feat[s, half] = feat_ref[s, 120:, 128 * half : 128 * half + 128].astype(F32)
    mr_rows(feat_ref, stream_ref, taps_ref, spec_ref, fwd_ref, inv_ref, out_ref, feat, prod, sums,
            2 * B, blocks)

    @pl.when(step == pl.num_programs(0) - 1)
    def _():
        for b in range(blocks):
            sum_ref[b] = put_row_sums(sums[b * B : (b + 1) * B, :], B)


def mr_upper(feat, stream_in, taps, spec, forward, inverse):
    rows, chans = stream_in.shape
    blocks = rows // B - 2
    return pl.pallas_call(
        functools.partial(upper_kernel, blocks=blocks),
        grid=(chans // 256,),
        in_specs=[
            pl.BlockSpec((3, rows, 256), lambda c: (0, 0, c)),
            pl.BlockSpec((rows, 256), lambda c: (0, c)),
            pl.BlockSpec((3, 7, 256), lambda c: (0, 0, c)),
            pl.BlockSpec((2, B, 256), lambda c: (0, 0, c)),
            pl.BlockSpec((2 * B, 2 * B), lambda c: (0, 0)),
            pl.BlockSpec((B, 2 * B), lambda c: (0, 0)),
        ],
        out_specs=[
            pl.BlockSpec((blocks * B, 256), lambda c: (0, c)),
            pl.BlockSpec((blocks, 8, 128), lambda c: (0, 0, 0)),
        ],
        out_shape=[
            pltpu.HBM((blocks * B, chans), F32),
            jax.ShapeDtypeStruct((blocks, 8, 128), F32),
        ],
        scratch_shapes=[
            pltpu.VMEM((3, 2, rows - 120, 128), F32),
            pltpu.VMEM(((blocks + 1) * B, 256), BF16),
            pltpu.VMEM((blocks * B, 128), F32),
        ],
        compiler_params=params(20),
        cost_estimate=cost(2 * 10**9, 14 * 10**6),
        name="mr_upper",
    )(feat, stream_in, taps, spec, forward, inverse)


def lower_kernel(feat_ref, stream_ref, taps_ref, spec_ref, fwd_ref, inv_ref, halo_ref, upper_ref,
                 out_ref, sum_ref, feat, prod, sums, *, blocks):
    step = pl.program_id(0)

    @pl.when(step == 0)
    def _():
        sums[...] = jnp.zeros_like(sums)

    for half in range(2):
        lanes = slice(128 * half, 128 * half + 128)
        for s in range(3):
            feat[s, half, 0:8] = halo_ref[128 + 8 * s : 136 + 8 * s, lanes].astype(F32)
            feat[s, half, 8:] = feat_ref[s, :, lanes].astype(F32)
        before = halo_ref[152:160, lanes].astype(F32) + halo_ref[160:168, lanes].astype(F32)
        sums[2 * B : 2 * B + 8, :] += before * before
    prod[0:B, :] = halo_ref[0:B, :]
    mr_rows(feat_ref, stream_ref, taps_ref, spec_ref, fwd_ref, inv_ref, out_ref, feat, prod, sums,
            0, 2)

    @pl.when(step == pl.num_programs(0) - 1)
    def _():
        for b in range(3):
            sum_ref[b] = put_row_sums(sums[b * B : (b + 1) * B, :], B)
        sum_ref[3:] = upper_ref[...]


def mr_lower(feat, stream_in, taps, spec, forward, inverse, halo, upper):
    rows, chans = stream_in.shape
    blocks = upper.shape[0]
    return pl.pallas_call(
        functools.partial(lower_kernel, blocks=blocks),
        grid=(chans // 256,),
        in_specs=[
            pl.BlockSpec((3, 2 * B, 256), lambda c: (0, 0, c)),
            pl.BlockSpec((2 * B, 256), lambda c: (0, c)),
            pl.BlockSpec((3, 7, 256), lambda c: (0, 0, c)),
            pl.BlockSpec((2, B, 256), lambda c: (0, 0, c)),
            pl.BlockSpec((2 * B, 2 * B), lambda c: (0, 0)),
            pl.BlockSpec((B, 2 * B), lambda c: (0, 0)),
            pl.BlockSpec((168, 256), lambda c: (0, c)),
            pl.BlockSpec((blocks, 8, 128), lambda c: (0, 0, 0)),
        ],
        out_specs=[
            pl.BlockSpec((2 * B, 256), lambda c: (0, c)),
            pl.BlockSpec((blocks + 3, 8, 128), lambda c: (0, 0, 0)),
        ],
        out_shape=[
            pltpu.HBM((2 * B, chans), F32),
            jax.ShapeDtypeStruct((blocks + 3, 8, 128), F32),
        ],
        scratch_shapes=[
            pltpu.VMEM((3, 2, 2 * B + 8, 128), F32),
            pltpu.VMEM((3 * B, 256), BF16),
            pltpu.VMEM((3 * B, 128), F32),
        ],
        compiler_params=params(14),
        cost_estimate=cost(7 * 10**8, 4 * 10**6),
        name="mr_lower",
    )(feat, stream_in, taps, spec, forward, inverse, halo, upper)


def state_kernel(low_ref, up_ref, halo_ref, s0_ref, s1_ref, s2_ref, s3_ref, gain_ref, taps_ref,
                 q8_ref, qs_ref, normed_ref, prod_ref, state_ref, inv, rows_f32, *, blocks):
    step = pl.program_id(0)

    @pl.when(step == 0)
    def _():
        total = s0_ref[...] + s1_ref[...] + s2_ref[...] + s3_ref[...]
        scale = lax.rsqrt(total * (1.0 / D) + EPS)
        for b in range(blocks + 1):
            spread = jnp.broadcast_to(scale[b, 0:1, :], (B, B))
            inv[b * B : (b + 1) * B, :] = jnp.transpose(spread)

    gain = gain_ref[...]
    before = halo_ref[0:8, :].astype(F32) + halo_ref[8:16, :].astype(F32)
    before = (before * inv[2 * B : 2 * B + 8, :] * gain).astype(BF16)
    normed_ref[0:8, :] = before
    rows_f32[0:8, :] = before.astype(F32)
    acc = [jnp.zeros((8, 128), F32) for _ in range(MODES)]
    q8 = [jnp.broadcast_to(q8_ref[n : n + 1, :], (8, 128)) for n in range(MODES)]
    for b in range(blocks):
        if b < 2:
            x = low_ref[b * B : (b + 1) * B, :]
            scale = inv[b * B : (b + 1) * B, :]
        else:
            x = up_ref[(b - 2) * B : (b - 1) * B, :]
            scale = inv[(b + 1) * B : (b + 2) * B, :]
        normed = (x * scale * gain).astype(BF16)
        start = 8 + b * B
        normed_ref[start : start + B, :] = normed
        rows_f32[start : start + B, :] = normed.astype(F32)
        keys = conv7(rows_f32, taps_ref[1], start, B)
        vals = conv7(rows_f32, taps_ref[2], start, B)
        product = (keys * vals).astype(BF16)
        prod_ref[b * B : (b + 1) * B, :] = product
        wide = product.astype(F32)
        for i in range(B // 8):
            part = wide[8 * i : 8 * i + 8]
            acc = [a * q + part for a, q in zip(acc, q8)]
        for n in range(MODES):
            state_ref[b, n : n + 1, :] = jnp.sum(acc[n] * qs_ref[n], axis=0, keepdims=True)


def li_states(low, up, halo, sums, gain, taps, q8, qs):
    chans = low.shape[1]
    rows = low.shape[0] + up.shape[0]
    blocks = rows // B
    sum_spec = pl.BlockSpec(sums[0].shape, lambda c: (0, 0, 0))
    return pl.pallas_call(
        functools.partial(state_kernel, blocks=blocks),
        grid=(chans // 128,),
        in_specs=[
            pl.BlockSpec((2 * B, 128), lambda c: (0, c)),
            pl.BlockSpec((rows - 2 * B, 128), lambda c: (0, c)),
            pl.BlockSpec((16, 128), lambda c: (0, c)),
            sum_spec, sum_spec, sum_spec, sum_spec,
            pl.BlockSpec((1, 128), lambda c: (0, c)),
            pl.BlockSpec((3, 7, 128), lambda c: (0, 0, c)),
            pl.BlockSpec((MODES, 128), lambda c: (0, c)),
            pl.BlockSpec((MODES, 8, 128), lambda c: (0, 0, c)),
        ],
        out_specs=[
            pl.BlockSpec((8 + rows, 128), lambda c: (0, c)),
            pl.BlockSpec((rows, 128), lambda c: (0, c)),
            pl.BlockSpec((blocks, MODES, 128), lambda c: (0, 0, c)),
        ],
        out_shape=[
            pltpu.HBM((8 + rows, chans), BF16),
            pltpu.HBM((rows, chans), BF16),
            jax.ShapeDtypeStruct((blocks, MODES, chans), F32),
        ],
        scratch_shapes=[
            pltpu.VMEM(((blocks + 1) * B, 128), F32),
            pltpu.VMEM((8 + rows, 128), F32),
        ],
        compiler_params=params(14),
        cost_estimate=cost(90 * 10**6, 9 * 10**6),
        name="li_states",
    )(*in_hbm(low, up), halo, *sums, gain, taps, q8, qs)


def near_kernel(low_ref, up_ref, normed_ref, prod_ref, taps_ref, spec_ref, fwd_ref, inv_ref,
                base_ref, gate_ref, rows_f32, *, blocks):
    forward, inverse = fwd_ref[...], inv_ref[...]
    for half in range(2):
        rows_f32[half] = normed_ref[:, 128 * half : 128 * half + 128].astype(F32)
    for b in range(blocks):
        rows = slice(b * B, (b + 1) * B)
        near = spectral(prod_ref[rows, :], forward, spec_ref[0], spec_ref[1], inverse)
        for half in range(2):
            lanes = slice(128 * half, 128 * half + 128)
            gate = conv7(rows_f32.at[half], taps_ref[0, :, lanes], 8 + b * B, B)
            stream = low_ref[rows, lanes] if b < 2 else up_ref[(b - 2) * B : (b - 1) * B, lanes]
            base_ref[rows, lanes] = stream + gate * near[:, lanes]
            gate_ref[rows, lanes] = gate


def li_near(low, up, normed, product, taps, spec, forward, inverse, part, parts):
    rows, chans = product.shape
    steps = chans // 256 // parts
    at = part * steps
    return pl.pallas_call(
        functools.partial(near_kernel, blocks=rows // B),
        grid=(steps,),
        in_specs=[
            pl.BlockSpec((2 * B, 256), lambda c: (0, at + c)),
            pl.BlockSpec((rows - 2 * B, 256), lambda c: (0, at + c)),
            pl.BlockSpec((8 + rows, 256), lambda c: (0, at + c)),
            pl.BlockSpec((rows, 256), lambda c: (0, at + c)),
            pl.BlockSpec((3, 7, 256), lambda c: (0, 0, at + c)),
            pl.BlockSpec((2, B, 256), lambda c: (0, 0, at + c)),
            pl.BlockSpec((2 * B, B), lambda c: (0, 0)),
            pl.BlockSpec((B, 2 * B), lambda c: (0, 0)),
        ],
        out_specs=[
            pl.BlockSpec((rows, 256), lambda c: (0, c)),
            pl.BlockSpec((rows, 256), lambda c: (0, c)),
        ],
        out_shape=[pltpu.HBM((rows, steps * 256), F32)] * 2,
        scratch_shapes=[pltpu.VMEM((2, 8 + rows, 128), F32)],
        compiler_params=params(16),
        cost_estimate=cost(10**9 // parts, 16 * 10**6 // parts),
        name="li_near",
    )(*in_hbm(low, up, normed, product), taps, spec, forward, inverse)


def far_kernel(base0_ref, gate0_ref, base1_ref, gate1_ref, state_ref, in_ref, q8_ref, q128_ref,
               wq_ref, out_ref, *, blocks, half):
    step = pl.program_id(0)
    operands = (state_ref, in_ref, q8_ref, q128_ref, wq_ref, out_ref, blocks)

    @pl.when(step < half)
    def _():
        far_rows(base0_ref, gate0_ref, *operands)

    @pl.when(step >= half)
    def _():
        far_rows(base1_ref, gate1_ref, *operands)


def far_rows(base_ref, gate_ref, state_ref, in_ref, q8_ref, q128_ref, wq_ref, out_ref, blocks):
    q8 = [jnp.broadcast_to(q8_ref[n : n + 1, :], (8, 128)) for n in range(MODES)]
    incoming = in_ref[...]
    for b in range(blocks):
        here = incoming if b == 0 else incoming + state_ref[b - 1]
        incoming = incoming * q128_ref[...]
        modes = [wq_ref[n] * here[n : n + 1, :] for n in range(MODES)]
        for i in range(B // 8):
            level = modes
            while len(level) > 1:
                level = [a + c for a, c in zip(level[::2], level[1::2])]
            rows = slice(b * B + 8 * i, b * B + 8 * i + 8)
            out_ref[rows, :] = (base_ref[rows, :] + gate_ref[rows, :] * level[0]).astype(BF16)
            if i < B // 8 - 1:
                modes = [m * q for m, q in zip(modes, q8)]


def li_far(nears, states, incoming, q8, q128, wq):
    rows = nears[0][0].shape[0]
    chans = states.shape[2]
    blocks = rows // B
    half = chans // 256
    first = pl.BlockSpec((rows, 128), lambda c: (0, jnp.minimum(c, half - 1)))
    second = pl.BlockSpec((rows, 128), lambda c: (0, jnp.maximum(c - half, 0)))
    return pl.pallas_call(
        functools.partial(far_kernel, blocks=blocks, half=half),
        grid=(chans // 128,),
        in_specs=[
            first, first, second, second,
            pl.BlockSpec((blocks, MODES, 128), lambda c: (0, 0, c)),
            pl.BlockSpec((MODES, 128), lambda c: (0, c)),
            pl.BlockSpec((MODES, 128), lambda c: (0, c)),
            pl.BlockSpec((MODES, 128), lambda c: (0, c)),
            pl.BlockSpec((MODES, 8, 128), lambda c: (0, 0, c)),
        ],
        out_specs=pl.BlockSpec((rows, 128), lambda c: (0, c)),
        out_shape=jax.ShapeDtypeStruct((rows, chans), BF16),
        compiler_params=params(12),
        cost_estimate=cost(70 * 10**6, 10 * 10**6),
        name="li_far",
    )(*in_hbm(*nears[0], *nears[1]), states, incoming, q8, q128, wq)


def to_next(value):
    lines, places = lax.axis_size("line"), lax.axis_size("place")
    count = lines * places
    return lax.ppermute(value, ("line", "place"), [(i, i + 1) for i in range(count - 1)])


def to_all(value, axis):
    count = lax.axis_size(axis)
    copies = jnp.broadcast_to(value.astype(BF16)[None], (count,) + value.shape)
    return lax.all_to_all(copies, axis, 0, 0)


def weighted(parts, rates, span, upto):
    steps = upto - 1 - jnp.arange(parts.shape[0], dtype=jnp.int32)
    ages = jnp.maximum(steps, 0).astype(F32)[:, None, None] * float(span)
    terms = jnp.exp(-rates[None] * ages) * parts.astype(F32)
    return jnp.sum(jnp.where(steps[:, None, None] >= 0, terms, 0.0), axis=0)


def body(stream_in, features, mr_taps, mr_filter, norm_gain, li_taps, modal_rates, modal_weights):
    rows = stream_in.shape[0]
    feat, stream_in = in_hbm(jnp.transpose(features, (1, 0, 2)), stream_in)
    mr_t = jnp.transpose(mr_taps, (0, 2, 1))
    li_t = jnp.transpose(li_taps, (0, 2, 1))
    rates = jnp.transpose(modal_rates)
    weights = jnp.transpose(modal_weights)
    gain = norm_gain[None, :]
    fwd_np, inv_np = dft_tables()
    forward = jnp.asarray(fwd_np, BF16)
    inverse = jnp.asarray(inv_np, BF16)
    half_fwd = jnp.asarray(fwd_np[:, :B], F32)

    near_high = fwd_np[:, :B].astype(BF16)
    near_low = (fwd_np[:, :B] - near_high.astype(np.float64)).astype(BF16)
    split_fwd = jnp.asarray(np.concatenate([near_high, near_low], axis=1))
    bundle, mr_spec = mr_tail(feat, stream_in, mr_t, mr_filter, split_fwd)
    halo = to_next(bundle)
    up, up_sums = mr_upper(feat, stream_in, mr_t, mr_spec, forward, inverse[B:])
    low, own = mr_lower(feat, stream_in, mr_t, mr_spec, forward, inverse[B:], halo, up_sums)
    ways = lax.axis_size("tp")
    sums = [own] + [
        lax.ppermute(own, "tp", [(i, (i + k) % ways) for i in range(ways)]) for k in range(1, ways)
    ]

    rates, weights, own = lax.optimization_barrier((rates, weights, own))
    scaled = weights * jnp.sqrt(1.0 - jnp.exp(-2.0 * rates))
    lags = jnp.arange(B, dtype=F32)
    near_taps = jnp.sum(scaled[None] * jnp.exp(-rates[None] * lags[:, None, None]), axis=1)
    li_spec = jnp.dot(half_fwd, near_taps, precision=HIGH).reshape(2, B, -1)
    within = jnp.arange(8, dtype=F32)[None, :, None]
    q8 = jnp.exp(-8.0 * rates)
    q128 = jnp.exp(-float(B) * rates)
    qs = jnp.exp(-rates[:, None, :] * (7.0 - within))
    wq = scaled[:, None, :] * jnp.exp(-rates[:, None, :] * (within + 1.0))

    gain, li_spec, wq, q128 = lax.optimization_barrier((gain, li_spec, wq, q128))
    normed, product, states = li_states(low, up, halo[152:168], sums, gain, li_t, q8, qs)
    near_args = (normed, product, li_t, li_spec, forward[:, :B], inverse[:B])
    place, line = lax.axis_index("place"), lax.axis_index("line")
    places = lax.axis_size("place")
    with jax.named_scope("scan_places"):
        parts = to_all(states[-1], "place")
    first = li_near(low, up, *near_args, 0, 2)
    with jax.named_scope("scan_places"):
        parts, first = lax.optimization_barrier((parts, first))
        whole = weighted(parts, rates, rows, places)
        prefix = weighted(parts, rates, rows, place)
    with jax.named_scope("scan_lines"):
        parts = to_all(whole, "line")
    normed, whole = lax.optimization_barrier((normed, whole))
    second = li_near(low, up, normed, *near_args[1:], 1, 2)
    with jax.named_scope("scan_lines"):
        parts, second = lax.optimization_barrier((parts, second))
        before = weighted(parts, rates, rows * places, line)
        incoming = prefix + before * jnp.exp(-rates * (rows * place.astype(F32)))
    return li_far((first, second), states, incoming, q8, q128, wq)


def solution(mesh):
    ctx, tp = mesh.devices.shape
    places = 8 if ctx % 8 == 0 else ctx
    split = jax.sharding.Mesh(
        mesh.devices.reshape(ctx // places, places, tp), ("line", "place", "tp")
    )
    seq = ("line", "place")
    in_specs = (
        P(seq, "tp"),
        P(seq, None, "tp"),
        P(None, "tp", None),
        P("tp", None),
        P("tp"),
        P(None, "tp", None),
        P("tp", None),
        P("tp", None),
    )
    return jax.shard_map(
        body, mesh=split, in_specs=in_specs, out_specs=P(seq, "tp"), check_vma=False
    )
```

```python
import functools

import jax
import jax.numpy as jnp
import numpy as np
from jax import lax
from jax.experimental import pallas as pl
from jax.experimental.pallas import tpu as pltpu
from jax.sharding import PartitionSpec as P

D = 4096
EPS = 1e-06
MODES = 16
B = 128
MR_GROUP = 2
LI_GROUP = 2
HIGH = lax.Precision.HIGHEST
F32 = jnp.float32
BF16 = jnp.bfloat16


def dft_tables():
    j = np.arange(2 * B)
    k = np.arange(B)
    angle = np.pi * (2 * k[:, None] + 1) * j[None, :] / (2 * B)
    cos, sin = np.cos(angle), np.sin(angle)
    forward = np.concatenate([cos, -sin], axis=0)
    inverse = np.concatenate([cos.T, -sin.T], axis=1) / B
    return forward, inverse


def params(mib):
    return pltpu.CompilerParams(vmem_limit_bytes=mib * 2**20)


def in_hbm(*values):
    return [pltpu.with_memory_space_constraint(value, pltpu.HBM) for value in values]


def cost(flops, bytes_accessed):
    return pl.CostEstimate(flops=flops, bytes_accessed=bytes_accessed, transcendentals=0)


def conv7(rows_ref, taps, start, count):
    total = taps[0:1] * rows_ref[pl.ds(start, count), :]
    for tap in range(1, 7):
        total = total + taps[tap : tap + 1] * rows_ref[pl.ds(start - tap, count), :]
    return total


def tail_kernel(feat_ref, stream_ref, taps_ref, filt_ref, fwd_ref, out_ref, spec_ref, feat, prod, filt):
    n_in, n_prod = 160, 144
    first = 256 - n_in
    turned = jnp.transpose(filt_ref[...].astype(F32))
    filt[...] = turned
    twice = jnp.concatenate([turned, turned], axis=0).astype(BF16)
    spec = jnp.dot(fwd_ref[...], twice, preferred_element_type=F32)
    spec_ref[0] = spec[:B]
    spec_ref[1] = spec[B:]
    for half in range(2):
        lanes = slice(128 * half, 128 * half + 128)
        for s in range(3):
            feat[s] = feat_ref[s, first:256, lanes].astype(F32)
        keys = conv7(feat.at[1], taps_ref[1, :, lanes], 16, n_prod)
        vals = conv7(feat.at[2], taps_ref[2, :, lanes], 16, n_prod)
        product = (keys * vals).astype(BF16)
        prod[...] = product.astype(F32)
        medium = jnp.zeros((8, 128), F32)
        for lag in range(128):
            medium = medium + filt[lag : lag + 1, lanes] * prod[pl.ds(136 - lag, 8), :]
        gate = conv7(feat.at[0], taps_ref[0, :, lanes], n_in - 8, 8)
        stream = stream_ref[8:16, lanes].astype(F32) + gate * medium
        high = stream.astype(BF16)
        out_ref[0:128, lanes] = product[16:144]
        for s in range(3):
            out_ref[128 + 8 * s : 136 + 8 * s, lanes] = feat_ref[s, 248:256, lanes]
        out_ref[152:160, lanes] = high
        out_ref[160:168, lanes] = (stream - high.astype(F32)).astype(BF16)


def mr_tail(feat, stream_in, taps, filt, forward):
    rows, chans = stream_in.shape
    last = rows // 256 - 1
    end = rows // 16 - 1
    return pl.pallas_call(
        tail_kernel,
        grid=(chans // 256,),
        in_specs=[
            pl.BlockSpec((3, 256, 256), lambda c: (0, last, c)),
            pl.BlockSpec((16, 256), lambda c: (end, c)),
            pl.BlockSpec((3, 7, 256), lambda c: (0, 0, c)),
            pl.BlockSpec((256, 128), lambda c: (c, 0)),
            pl.BlockSpec((2 * B, 2 * B), lambda c: (0, 0)),
        ],
        out_specs=[
            pl.BlockSpec((168, 256), lambda c: (0, c)),
            pl.BlockSpec((2, B, 256), lambda c: (0, 0, c)),
        ],
        out_shape=[
            jax.ShapeDtypeStruct((168, chans), BF16),
            jax.ShapeDtypeStruct((2, B, chans), F32),
        ],
        scratch_shapes=[
            pltpu.VMEM((3, 160, 128), F32),
            pltpu.VMEM((144, 128), F32),
            pltpu.VMEM((128, 256), F32),
        ],
        compiler_params=params(12),
        cost_estimate=cost(20 * 10**6, 2 * 10**6),
        name="mr_tail",
    )(feat, stream_in, *in_hbm(taps, filt, forward))


def spectral(windows, forward, real, imag, inverse):
    count, width = len(windows), windows[0].shape[1]
    spec = jnp.dot(forward, jnp.concatenate(windows, axis=1), preferred_element_type=F32)
    xr, xi = spec[:B], spec[B:]
    real = jnp.concatenate([real] * count, axis=1)
    imag = jnp.concatenate([imag] * count, axis=1)
    out = jnp.concatenate([xr * real - xi * imag, xr * imag + xi * real], axis=0)
    found = jnp.dot(inverse, out.astype(BF16), preferred_element_type=F32)
    return [found[:, width * i : width * (i + 1)] for i in range(count)]


def put_row_sums(squares, count):
    ones = jnp.ones((8, 128), F32)
    return lax.dot_general(
        ones, squares, (((1,), (1,)), ((), ())), precision=HIGH, preferred_element_type=F32
    )


def mr_rows(feat_ref, stream_ref, taps_ref, spec_ref, fwd_ref, inv_ref, out_ref, feat, prod, sums,
            first, blocks):
    forward, inverse = fwd_ref[...], inv_ref[...]

    def make_product(b):
        start = 8 + (b - 1) * B if first == 0 else 8 + b * B
        for half in range(2):
            lanes = slice(128 * half, 128 * half + 128)
            keys = conv7(feat.at[1, half], taps_ref[1, :, lanes], start, B)
            vals = conv7(feat.at[2, half], taps_ref[2, :, lanes], start, B)
            prod[b * B : (b + 1) * B, lanes] = (keys * vals).astype(BF16)

    for b in range(1 if first == 0 else 0, MR_GROUP + 1):
        make_product(b)
    for group in range(0, blocks, MR_GROUP):
        windows = [prod[i * B : (i + 2) * B, :] for i in range(group, group + MR_GROUP)]
        found = spectral(windows, forward, spec_ref[0], spec_ref[1], inverse)
        for b in range(group + MR_GROUP + 1, min(group + 2 * MR_GROUP, blocks) + 1):
            make_product(b)
        for b in range(group, group + MR_GROUP):
            rows = slice(b * B, (b + 1) * B)
            start = 8 + b * B if first == 0 else 8 + (b + 1) * B
            for half in range(2):
                lanes = slice(128 * half, 128 * half + 128)
                gate = conv7(feat.at[0, half], taps_ref[0, :, lanes], start, B)
                stream = stream_ref[first + b * B : first + (b + 1) * B, lanes].astype(F32)
                stream = stream + gate * found[b - group][:, lanes]
                out_ref[rows, lanes] = stream
                sums[rows, :] += stream * stream


def upper_kernel(feat_ref, stream_ref, taps_ref, spec_ref, fwd_ref, inv_ref, out_ref, sum_ref,
                 feat, prod, sums, *, blocks):
    step = pl.program_id(0)

    @pl.when(step == 0)
    def _():
        sums[...] = jnp.zeros_like(sums)

    for s in range(3):
        for half in range(2):
            feat[s, half] = feat_ref[s, 120:, 128 * half : 128 * half + 128].astype(F32)
    mr_rows(feat_ref, stream_ref, taps_ref, spec_ref, fwd_ref, inv_ref, out_ref, feat, prod, sums,
            2 * B, blocks)

    @pl.when(step == pl.num_programs(0) - 1)
    def _():
        for b in range(blocks):
            sum_ref[b] = put_row_sums(sums[b * B : (b + 1) * B, :], B)


def mr_upper(feat, stream_in, taps, spec, forward, inverse):
    rows, chans = stream_in.shape
    blocks = rows // B - 2
    return pl.pallas_call(
        functools.partial(upper_kernel, blocks=blocks),
        grid=(chans // 256,),
        in_specs=[
            pl.BlockSpec((3, rows, 256), lambda c: (0, 0, c)),
            pl.BlockSpec((rows, 256), lambda c: (0, c)),
            pl.BlockSpec((3, 7, 256), lambda c: (0, 0, c)),
            pl.BlockSpec((2, B, 256), lambda c: (0, 0, c)),
            pl.BlockSpec((2 * B, 2 * B), lambda c: (0, 0)),
            pl.BlockSpec((B, 2 * B), lambda c: (0, 0)),
        ],
        out_specs=[
            pl.BlockSpec((blocks * B, 256), lambda c: (0, c)),
            pl.BlockSpec((blocks, 8, 128), lambda c: (0, 0, 0)),
        ],
        out_shape=[
            pltpu.HBM((blocks * B, chans), F32),
            jax.ShapeDtypeStruct((blocks, 8, 128), F32),
        ],
        scratch_shapes=[
            pltpu.VMEM((3, 2, rows - 120, 128), F32),
            pltpu.VMEM(((blocks + 1) * B, 256), BF16),
            pltpu.VMEM((blocks * B, 128), F32),
        ],
        compiler_params=params(20),
        cost_estimate=cost(2 * 10**9, 14 * 10**6),
        name="mr_upper",
    )(feat, stream_in, taps, spec, forward, inverse)


def lower_kernel(feat_ref, stream_ref, taps_ref, spec_ref, fwd_ref, inv_ref, halo_ref, upper_ref,
                 out_ref, sum_ref, feat, prod, sums, *, blocks):
    step = pl.program_id(0)

    @pl.when(step == 0)
    def _():
        sums[...] = jnp.zeros_like(sums)

    for half in range(2):
        lanes = slice(128 * half, 128 * half + 128)
        for s in range(3):
            feat[s, half, 0:8] = halo_ref[128 + 8 * s : 136 + 8 * s, lanes].astype(F32)
            feat[s, half, 8:] = feat_ref[s, :, lanes].astype(F32)
        before = halo_ref[152:160, lanes].astype(F32) + halo_ref[160:168, lanes].astype(F32)
        sums[2 * B : 2 * B + 8, :] += before * before
    prod[0:B, :] = halo_ref[0:B, :]
    mr_rows(feat_ref, stream_ref, taps_ref, spec_ref, fwd_ref, inv_ref, out_ref, feat, prod, sums,
            0, 2)

    @pl.when(step == pl.num_programs(0) - 1)
    def _():
        for b in range(3):
            sum_ref[b] = put_row_sums(sums[b * B : (b + 1) * B, :], B)
        sum_ref[3:] = upper_ref[...]


def mr_lower(feat, stream_in, taps, spec, forward, inverse, halo, upper):
    rows, chans = stream_in.shape
    blocks = upper.shape[0]
    return pl.pallas_call(
        functools.partial(lower_kernel, blocks=blocks),
        grid=(chans // 256,),
        in_specs=[
            pl.BlockSpec((3, 2 * B, 256), lambda c: (0, 0, c)),
            pl.BlockSpec((2 * B, 256), lambda c: (0, c)),
            pl.BlockSpec((3, 7, 256), lambda c: (0, 0, c)),
            pl.BlockSpec((2, B, 256), lambda c: (0, 0, c)),
            pl.BlockSpec((2 * B, 2 * B), lambda c: (0, 0)),
            pl.BlockSpec((B, 2 * B), lambda c: (0, 0)),
            pl.BlockSpec((168, 256), lambda c: (0, c)),
            pl.BlockSpec((blocks, 8, 128), lambda c: (0, 0, 0)),
        ],
        out_specs=[
            pl.BlockSpec((2 * B, 256), lambda c: (0, c)),
            pl.BlockSpec((blocks + 3, 8, 128), lambda c: (0, 0, 0)),
        ],
        out_shape=[
            pltpu.HBM((2 * B, chans), F32),
            jax.ShapeDtypeStruct((blocks + 3, 8, 128), F32),
        ],
        scratch_shapes=[
            pltpu.VMEM((3, 2, 2 * B + 8, 128), F32),
            pltpu.VMEM((3 * B, 256), BF16),
            pltpu.VMEM((3 * B, 128), F32),
        ],
        compiler_params=params(14),
        cost_estimate=cost(7 * 10**8, 4 * 10**6),
        name="mr_lower",
    )(feat, stream_in, taps, spec, forward, inverse, halo, upper)


def state_kernel(low_ref, up_ref, halo_ref, s0_ref, s1_ref, s2_ref, s3_ref, gain_ref, taps_ref,
                 q8_ref, qs_ref, normed_ref, prod_ref, state_ref, inv, rows_f32, *, blocks):
    step = pl.program_id(0)

    @pl.when(step == 0)
    def _():
        total = s0_ref[...] + s1_ref[...] + s2_ref[...] + s3_ref[...]
        scale = lax.rsqrt(total * (1.0 / D) + EPS)
        for b in range(blocks + 1):
            spread = jnp.broadcast_to(scale[b, 0:1, :], (B, B))
            inv[b * B : (b + 1) * B, :] = jnp.transpose(spread)

    gain = gain_ref[...]
    before = halo_ref[0:8, :].astype(F32) + halo_ref[8:16, :].astype(F32)
    before = (before * inv[2 * B : 2 * B + 8, :] * gain).astype(BF16)
    normed_ref[0:8, :] = before
    rows_f32[0:8, :] = before.astype(F32)
    acc = [jnp.zeros((8, 128), F32) for _ in range(MODES)]
    q8 = [jnp.broadcast_to(q8_ref[n : n + 1, :], (8, 128)) for n in range(MODES)]
    for b in range(blocks):
        if b < 2:
            x = low_ref[b * B : (b + 1) * B, :]
            scale = inv[b * B : (b + 1) * B, :]
        else:
            x = up_ref[(b - 2) * B : (b - 1) * B, :]
            scale = inv[(b + 1) * B : (b + 2) * B, :]
        normed = (x * scale * gain).astype(BF16)
        start = 8 + b * B
        normed_ref[start : start + B, :] = normed
        rows_f32[start : start + B, :] = normed.astype(F32)
        keys = conv7(rows_f32, taps_ref[1], start, B)
        vals = conv7(rows_f32, taps_ref[2], start, B)
        product = (keys * vals).astype(BF16)
        prod_ref[b * B : (b + 1) * B, :] = product
        wide = product.astype(F32)
        for i in range(B // 8):
            part = wide[8 * i : 8 * i + 8]
            acc = [a * q + part for a, q in zip(acc, q8)]
        for n in range(MODES):
            state_ref[b, n : n + 1, :] = jnp.sum(acc[n] * qs_ref[n], axis=0, keepdims=True)


def li_states(low, up, halo, sums, gain, taps, q8, qs):
    chans = low.shape[1]
    rows = low.shape[0] + up.shape[0]
    blocks = rows // B
    sum_spec = pl.BlockSpec(sums[0].shape, lambda c: (0, 0, 0))
    return pl.pallas_call(
        functools.partial(state_kernel, blocks=blocks),
        grid=(chans // 128,),
        in_specs=[
            pl.BlockSpec((2 * B, 128), lambda c: (0, c)),
            pl.BlockSpec((rows - 2 * B, 128), lambda c: (0, c)),
            pl.BlockSpec((16, 128), lambda c: (0, c)),
            sum_spec, sum_spec, sum_spec, sum_spec,
            pl.BlockSpec((1, 128), lambda c: (0, c)),
            pl.BlockSpec((3, 7, 128), lambda c: (0, 0, c)),
            pl.BlockSpec((MODES, 128), lambda c: (0, c)),
            pl.BlockSpec((MODES, 8, 128), lambda c: (0, 0, c)),
        ],
        out_specs=[
            pl.BlockSpec((8 + rows, 128), lambda c: (0, c)),
            pl.BlockSpec((rows, 128), lambda c: (0, c)),
            pl.BlockSpec((blocks, MODES, 128), lambda c: (0, 0, c)),
        ],
        out_shape=[
            pltpu.HBM((8 + rows, chans), BF16),
            pltpu.HBM((rows, chans), BF16),
            jax.ShapeDtypeStruct((blocks, MODES, chans), F32),
        ],
        scratch_shapes=[
            pltpu.VMEM(((blocks + 1) * B, 128), F32),
            pltpu.VMEM((8 + rows, 128), F32),
        ],
        compiler_params=params(14),
        cost_estimate=cost(90 * 10**6, 9 * 10**6),
        name="li_states",
    )(*in_hbm(low, up), halo, *sums, gain, taps, q8, qs)


def near_kernel(normed_ref, prod_ref, taps_ref, spec_ref, fwd_ref, inv_ref, *rest, blocks):
    near_ref, gate_ref, rows_f32 = rest[-3:]
    forward, inverse = fwd_ref[...], inv_ref[...]
    for half in range(2):
        rows_f32[half] = normed_ref[:, 128 * half : 128 * half + 128].astype(F32)
    for b in range(blocks):
        rows = slice(b * B, (b + 1) * B)
        if b % LI_GROUP == 0:
            windows = [prod_ref[i * B : (i + 1) * B, :] for i in range(b, b + LI_GROUP)]
            found = spectral(windows, forward, spec_ref[0], spec_ref[1], inverse)
        for half in range(2):
            lanes = slice(128 * half, 128 * half + 128)
            gate = conv7(rows_f32.at[half], taps_ref[0, :, lanes], 8 + b * B, B)
            gate_ref[rows, lanes] = gate.astype(BF16)
        near_ref[rows, :] = found[b % LI_GROUP].astype(BF16)


def li_near(normed, product, taps, spec, forward, inverse, part, parts, earlier=()):
    rows, chans = product.shape
    steps = chans // 256 // parts
    at = part * steps
    wide = pl.BlockSpec((rows, 256), lambda c: (0, at + c))
    return pl.pallas_call(
        functools.partial(near_kernel, blocks=rows // B),
        grid=(steps,),
        in_specs=[
            pl.BlockSpec((8 + rows, 256), lambda c: (0, at + c)),
            wide,
            pl.BlockSpec((3, 7, 256), lambda c: (0, 0, at + c)),
            pl.BlockSpec((2, B, 256), lambda c: (0, 0, at + c)),
            pl.BlockSpec((2 * B, B), lambda c: (0, 0)),
            pl.BlockSpec((B, 2 * B), lambda c: (0, 0)),
        ]
        + [pl.BlockSpec(memory_space=pl.ANY)] * len(earlier),
        out_specs=[wide, wide],
        out_shape=[pltpu.HBM((rows, chans), BF16)] * 2,
        scratch_shapes=[pltpu.VMEM((2, 8 + rows, 128), F32)],
        input_output_aliases={6 + i: i for i in range(len(earlier))},
        compiler_params=params(16),
        cost_estimate=cost(10**9 // parts, 8 * 10**6 // parts),
        name="li_near",
    )(*in_hbm(normed, product), taps, spec, forward, inverse, *in_hbm(*earlier))


def far_kernel(low_ref, up_ref, gate_ref, near_ref, state_ref, in_ref, q8_ref, q128_ref, wq_ref,
               out_ref, *, blocks):
    incoming = in_ref[...]
    for b in range(blocks):
        here = incoming if b == 0 else incoming + state_ref[b - 1]
        incoming = incoming * q128_ref[...]
        for half in range(2):
            lanes = slice(128 * half, 128 * half + 128)
            modes = [wq_ref[n, :, lanes] * here[n : n + 1, lanes] for n in range(MODES)]
            for i in range(B // 16):
                total = []
                for part in range(2):
                    level = modes
                    while len(level) > 1:
                        level = [a + c for a, c in zip(level[::2], level[1::2])]
                    total.append(level[0])
                    modes = [
                        m * jnp.broadcast_to(q8_ref[n : n + 1, lanes], (8, 128))
                        for n, m in enumerate(modes)
                    ]
                at = slice(b * B + 16 * i, b * B + 16 * i + 16)
                long = jnp.concatenate(total, axis=0) + near_ref[at, lanes].astype(F32)
                if b < 2:
                    stream = low_ref[at, lanes]
                else:
                    stream = up_ref[(b - 2) * B + 16 * i : (b - 2) * B + 16 * i + 16, lanes]
                gate = gate_ref[at, lanes].astype(F32)
                out_ref[at, lanes] = (stream + gate * long).astype(BF16)


def li_far(low, up, gate, near, states, incoming, q8, q128, wq):
    rows, chans = near.shape
    blocks = rows // B
    wide = pl.BlockSpec((rows, 256), lambda c: (0, c))
    modes = pl.BlockSpec((MODES, 256), lambda c: (0, c))
    return pl.pallas_call(
        functools.partial(far_kernel, blocks=blocks),
        grid=(chans // 256,),
        in_specs=[
            pl.BlockSpec((2 * B, 256), lambda c: (0, c)),
            pl.BlockSpec((rows - 2 * B, 256), lambda c: (0, c)),
            wide,
            wide,
            pl.BlockSpec((blocks, MODES, 256), lambda c: (0, 0, c)),
            modes,
            modes,
            modes,
            pl.BlockSpec((MODES, 8, 256), lambda c: (0, 0, c)),
        ],
        out_specs=wide,
        out_shape=jax.ShapeDtypeStruct((rows, chans), BF16),
        compiler_params=params(16),
        cost_estimate=cost(70 * 10**6, 12 * 10**6),
        name="li_far",
    )(*in_hbm(low, up, gate, near), states, incoming, q8, q128, wq)


def to_next(value):
    lines, places = lax.axis_size("line"), lax.axis_size("place")
    count = lines * places
    return lax.ppermute(value, ("line", "place"), [(i, i + 1) for i in range(count - 1)])


def to_all(value, axis):
    count = lax.axis_size(axis)
    copies = jnp.broadcast_to(value.astype(BF16)[None], (count,) + value.shape)
    return lax.all_to_all(copies, axis, 0, 0)


def weighted(parts, rates, span, upto):
    steps = upto - 1 - jnp.arange(parts.shape[0], dtype=jnp.int32)
    ages = jnp.maximum(steps, 0).astype(F32)[:, None, None] * float(span)
    terms = jnp.exp(-rates[None] * ages) * parts.astype(F32)
    return jnp.sum(jnp.where(steps[:, None, None] >= 0, terms, 0.0), axis=0)


def body(stream_in, features, mr_taps, mr_filter, norm_gain, li_taps, modal_rates, modal_weights):
    rows = stream_in.shape[0]
    feat, stream_in = in_hbm(jnp.transpose(features, (1, 0, 2)), stream_in)
    mr_t = jnp.transpose(mr_taps, (0, 2, 1))
    li_t = jnp.transpose(li_taps, (0, 2, 1))
    rates = jnp.transpose(modal_rates)
    weights = jnp.transpose(modal_weights)
    gain = norm_gain[None, :]
    fwd_np, inv_np = dft_tables()
    forward = jnp.asarray(fwd_np, BF16)
    inverse = jnp.asarray(inv_np, BF16)
    half_fwd = jnp.asarray(fwd_np[:, :B], F32)

    near_high = fwd_np[:, :B].astype(BF16)
    near_low = (fwd_np[:, :B] - near_high.astype(np.float64)).astype(BF16)
    split_fwd = jnp.asarray(np.concatenate([near_high, near_low], axis=1))
    bundle, mr_spec = mr_tail(feat, stream_in, mr_t, mr_filter, split_fwd)
    halo = to_next(bundle)
    up, up_sums = mr_upper(feat, stream_in, mr_t, mr_spec, forward, inverse[B:])
    low, own = mr_lower(feat, stream_in, mr_t, mr_spec, forward, inverse[B:], halo, up_sums)
    ways = lax.axis_size("tp")
    sums = [own] + [
        lax.ppermute(own, "tp", [(i, (i + k) % ways) for i in range(ways)]) for k in range(1, ways)
    ]

    rates, weights, own = lax.optimization_barrier((rates, weights, own))
    scaled = weights * jnp.sqrt(1.0 - jnp.exp(-2.0 * rates))
    lags = jnp.arange(B, dtype=F32)
    near_taps = jnp.sum(scaled[None] * jnp.exp(-rates[None] * lags[:, None, None]), axis=1)
    li_spec = jnp.dot(half_fwd, near_taps, precision=HIGH).reshape(2, B, -1)
    within = jnp.arange(8, dtype=F32)[None, :, None]
    q8 = jnp.exp(-8.0 * rates)
    q128 = jnp.exp(-float(B) * rates)
    qs = jnp.exp(-rates[:, None, :] * (7.0 - within))
    wq = scaled[:, None, :] * jnp.exp(-rates[:, None, :] * (within + 1.0))
    gain, li_spec, wq, q128 = lax.optimization_barrier((gain, li_spec, wq, q128))
    normed, product, states = li_states(low, up, halo[152:168], sums, gain, li_t, q8, qs)

    near_args = (li_t, li_spec, forward[:, :B], inverse[:B])
    place, line = lax.axis_index("place"), lax.axis_index("line")
    places = lax.axis_size("place")
    with jax.named_scope("scan_places"):
        parts = to_all(states[-1], "place")
    first = li_near(normed, product, *near_args, 0, 2)
    with jax.named_scope("scan_places"):
        parts, first = lax.optimization_barrier((parts, first))
        whole = weighted(parts, rates, rows, places)
        prefix = weighted(parts, rates, rows, place)
    with jax.named_scope("scan_lines"):
        parts = to_all(whole, "line")
    normed, whole = lax.optimization_barrier((normed, whole))
    near, gate = li_near(normed, product, *near_args, 1, 2, first)
    with jax.named_scope("scan_lines"):
        parts, near, gate = lax.optimization_barrier((parts, near, gate))
        before = weighted(parts, rates, rows * places, line)
        incoming = prefix + before * jnp.exp(-rates * (rows * place.astype(F32)))
    return li_far(low, up, gate, near, states, incoming, q8, q128, wq)


def solution(mesh):
    ctx, tp = mesh.devices.shape
    places = 8 if ctx % 8 == 0 else ctx
    split = jax.sharding.Mesh(
        mesh.devices.reshape(ctx // places, places, tp), ("line", "place", "tp")
    )
    seq = ("line", "place")
    in_specs = (
        P(seq, "tp"),
        P(seq, None, "tp"),
        P(None, "tp", None),
        P("tp", None),
        P("tp"),
        P(None, "tp", None),
        P("tp", None),
        P("tp", None),
    )
    return jax.shard_map(
        body, mesh=split, in_specs=in_specs, out_specs=P(seq, "tp"), check_vma=False
    )
```

```python
import functools

import jax
import jax.numpy as jnp
import numpy as np
from jax import lax
from jax.experimental import pallas as pl
from jax.experimental.pallas import tpu as pltpu
from jax.sharding import PartitionSpec as P

D = 4096
EPS = 1e-06
MODES = 16
B = 128
LI_GROUP = 2
HIGH = lax.Precision.HIGHEST
F32 = jnp.float32
BF16 = jnp.bfloat16


def dft_tables():
    j = np.arange(2 * B)
    k = np.arange(B)
    angle = np.pi * (2 * k[:, None] + 1) * j[None, :] / (2 * B)
    cos, sin = np.cos(angle), np.sin(angle)
    forward = np.concatenate([cos, -sin], axis=0)
    inverse = np.concatenate([cos.T, -sin.T], axis=1) / B
    return forward, inverse


def params(mib):
    return pltpu.CompilerParams(vmem_limit_bytes=mib * 2**20)


def in_hbm(*values):
    return [pltpu.with_memory_space_constraint(value, pltpu.HBM) for value in values]


def cost(flops, bytes_accessed):
    return pl.CostEstimate(flops=flops, bytes_accessed=bytes_accessed, transcendentals=0)


def conv7(rows_ref, taps, start, count):
    total = taps[0:1] * rows_ref[pl.ds(start, count), :]
    for tap in range(1, 7):
        total = total + taps[tap : tap + 1] * rows_ref[pl.ds(start - tap, count), :]
    return total


def tail_kernel(feat_ref, stream_ref, taps_ref, filt_ref, fwd_ref, out_ref, spec_ref, feat, prod, filt):
    n_in, n_prod = 160, 144
    first = 256 - n_in
    turned = jnp.transpose(filt_ref[...].astype(F32))
    filt[...] = turned
    twice = jnp.concatenate([turned, turned], axis=0).astype(BF16)
    spec = jnp.dot(fwd_ref[...], twice, preferred_element_type=F32)
    spec_ref[0] = spec[:B]
    spec_ref[1] = spec[B:]
    for half in range(2):
        lanes = slice(128 * half, 128 * half + 128)
        for s in range(3):
            feat[s] = feat_ref[s, first:256, lanes].astype(F32)
        keys = conv7(feat.at[1], taps_ref[1, :, lanes], 16, n_prod)
        vals = conv7(feat.at[2], taps_ref[2, :, lanes], 16, n_prod)
        product = (keys * vals).astype(BF16)
        prod[...] = product.astype(F32)
        medium = jnp.zeros((8, 128), F32)
        for lag in range(128):
            medium = medium + filt[lag : lag + 1, lanes] * prod[pl.ds(136 - lag, 8), :]
        gate = conv7(feat.at[0], taps_ref[0, :, lanes], n_in - 8, 8)
        stream = stream_ref[8:16, lanes].astype(F32) + gate * medium
        high = stream.astype(BF16)
        out_ref[0:128, lanes] = product[16:144]
        for s in range(3):
            out_ref[128 + 8 * s : 136 + 8 * s, lanes] = feat_ref[s, 248:256, lanes]
        out_ref[152:160, lanes] = high
        out_ref[160:168, lanes] = (stream - high.astype(F32)).astype(BF16)


def mr_tail(feat, stream_in, taps, filt, forward):
    rows, chans = stream_in.shape
    last = rows // 256 - 1
    end = rows // 16 - 1
    return pl.pallas_call(
        tail_kernel,
        grid=(chans // 256,),
        in_specs=[
            pl.BlockSpec((3, 256, 256), lambda c: (0, last, c)),
            pl.BlockSpec((16, 256), lambda c: (end, c)),
            pl.BlockSpec((3, 7, 256), lambda c: (0, 0, c)),
            pl.BlockSpec((256, 128), lambda c: (c, 0)),
            pl.BlockSpec((2 * B, 2 * B), lambda c: (0, 0)),
        ],
        out_specs=[
            pl.BlockSpec((168, 256), lambda c: (0, c)),
            pl.BlockSpec((2, B, 256), lambda c: (0, 0, c)),
        ],
        out_shape=[
            jax.ShapeDtypeStruct((168, chans), BF16),
            jax.ShapeDtypeStruct((2, B, chans), F32),
        ],
        scratch_shapes=[
            pltpu.VMEM((3, 160, 128), F32),
            pltpu.VMEM((144, 128), F32),
            pltpu.VMEM((128, 256), F32),
        ],
        compiler_params=params(12),
        cost_estimate=cost(20 * 10**6, 2 * 10**6),
        name="mr_tail",
    )(feat, stream_in, *in_hbm(taps, filt, forward))


def spectral(windows, forward, real, imag, inverse):
    count, width = len(windows), windows[0].shape[1]
    spec = jnp.dot(forward, jnp.concatenate(windows, axis=1), preferred_element_type=F32)
    xr, xi = spec[:B], spec[B:]
    real = jnp.concatenate([real] * count, axis=1)
    imag = jnp.concatenate([imag] * count, axis=1)
    out = jnp.concatenate([xr * real - xi * imag, xr * imag + xi * real], axis=0)
    found = jnp.dot(inverse, out.astype(BF16), preferred_element_type=F32)
    return [found[:, width * i : width * (i + 1)] for i in range(count)]


def put_row_sums(squares, count):
    ones = jnp.ones((8, 128), F32)
    return lax.dot_general(
        ones, squares, (((1,), (1,)), ((), ())), precision=HIGH, preferred_element_type=F32
    )


def mr_rows(feat_ref, stream_ref, taps_ref, spec_ref, fwd_ref, inv_ref, out_ref, feat, prod, sums,
            first, blocks):
    forward, inverse = fwd_ref[...], inv_ref[...]
    per = 3 if blocks % 3 == 0 else 2

    def make_product(b):
        start = 8 + (b - 1) * B if first == 0 else 8 + b * B
        for half in range(2):
            lanes = slice(128 * half, 128 * half + 128)
            keys = conv7(feat.at[1, half], taps_ref[1, :, lanes], start, B)
            vals = conv7(feat.at[2, half], taps_ref[2, :, lanes], start, B)
            prod[b * B : (b + 1) * B, lanes] = (keys * vals).astype(BF16)

    for b in range(1 if first == 0 else 0, per + 1):
        make_product(b)
    for group in range(0, blocks, per):
        windows = [prod[i * B : (i + 2) * B, :] for i in range(group, group + per)]
        found = spectral(windows, forward, spec_ref[0], spec_ref[1], inverse)
        for b in range(group + per + 1, min(group + 2 * per, blocks) + 1):
            make_product(b)
        for b in range(group, group + per):
            rows = slice(b * B, (b + 1) * B)
            start = 8 + b * B if first == 0 else 8 + (b + 1) * B
            for half in range(2):
                lanes = slice(128 * half, 128 * half + 128)
                gate = conv7(feat.at[0, half], taps_ref[0, :, lanes], start, B)
                stream = stream_ref[first + b * B : first + (b + 1) * B, lanes].astype(F32)
                stream = stream + gate * found[b - group][:, lanes]
                out_ref[rows, lanes] = stream
                sums[rows, :] += stream * stream


def upper_kernel(feat_ref, stream_ref, taps_ref, spec_ref, fwd_ref, inv_ref, out_ref, sum_ref,
                 feat, prod, sums, *, blocks):
    step = pl.program_id(0)

    @pl.when(step == 0)
    def _():
        sums[...] = jnp.zeros_like(sums)

    for s in range(3):
        for half in range(2):
            feat[s, half] = feat_ref[s, 120:, 128 * half : 128 * half + 128].astype(F32)
    mr_rows(feat_ref, stream_ref, taps_ref, spec_ref, fwd_ref, inv_ref, out_ref, feat, prod, sums,
            2 * B, blocks)

    @pl.when(step == pl.num_programs(0) - 1)
    def _():
        for b in range(blocks):
            sum_ref[b] = put_row_sums(sums[b * B : (b + 1) * B, :], B)


def mr_upper(feat, stream_in, taps, spec, forward, inverse):
    rows, chans = stream_in.shape
    blocks = rows // B - 2
    return pl.pallas_call(
        functools.partial(upper_kernel, blocks=blocks),
        grid=(chans // 256,),
        in_specs=[
            pl.BlockSpec((3, rows, 256), lambda c: (0, 0, c)),
            pl.BlockSpec((rows, 256), lambda c: (0, c)),
            pl.BlockSpec((3, 7, 256), lambda c: (0, 0, c)),
            pl.BlockSpec((2, B, 256), lambda c: (0, 0, c)),
            pl.BlockSpec((2 * B, 2 * B), lambda c: (0, 0)),
            pl.BlockSpec((B, 2 * B), lambda c: (0, 0)),
        ],
        out_specs=[
            pl.BlockSpec((blocks * B, 256), lambda c: (0, c)),
            pl.BlockSpec((blocks, 8, 128), lambda c: (0, 0, 0)),
        ],
        out_shape=[
            pltpu.HBM((blocks * B, chans), F32),
            jax.ShapeDtypeStruct((blocks, 8, 128), F32),
        ],
        scratch_shapes=[
            pltpu.VMEM((3, 2, rows - 120, 128), F32),
            pltpu.VMEM(((blocks + 1) * B, 256), BF16),
            pltpu.VMEM((blocks * B, 128), F32),
        ],
        compiler_params=params(20),
        cost_estimate=cost(2 * 10**9, 14 * 10**6),
        name="mr_upper",
    )(feat, stream_in, taps, spec, forward, inverse)


def lower_kernel(feat_ref, stream_ref, taps_ref, spec_ref, fwd_ref, inv_ref, halo_ref, upper_ref,
                 out_ref, sum_ref, feat, prod, sums, *, blocks):
    step = pl.program_id(0)

    @pl.when(step == 0)
    def _():
        sums[...] = jnp.zeros_like(sums)

    for half in range(2):
        lanes = slice(128 * half, 128 * half + 128)
        for s in range(3):
            feat[s, half, 0:8] = halo_ref[128 + 8 * s : 136 + 8 * s, lanes].astype(F32)
            feat[s, half, 8:] = feat_ref[s, :, lanes].astype(F32)
        before = halo_ref[152:160, lanes].astype(F32) + halo_ref[160:168, lanes].astype(F32)
        sums[2 * B : 2 * B + 8, :] += before * before
    prod[0:B, :] = halo_ref[0:B, :]
    mr_rows(feat_ref, stream_ref, taps_ref, spec_ref, fwd_ref, inv_ref, out_ref, feat, prod, sums,
            0, 2)

    @pl.when(step == pl.num_programs(0) - 1)
    def _():
        for b in range(3):
            sum_ref[b] = put_row_sums(sums[b * B : (b + 1) * B, :], B)
        sum_ref[3:] = upper_ref[...]


def mr_lower(feat, stream_in, taps, spec, forward, inverse, halo, upper):
    rows, chans = stream_in.shape
    blocks = upper.shape[0]
    return pl.pallas_call(
        functools.partial(lower_kernel, blocks=blocks),
        grid=(chans // 256,),
        in_specs=[
            pl.BlockSpec((3, 2 * B, 256), lambda c: (0, 0, c)),
            pl.BlockSpec((2 * B, 256), lambda c: (0, c)),
            pl.BlockSpec((3, 7, 256), lambda c: (0, 0, c)),
            pl.BlockSpec((2, B, 256), lambda c: (0, 0, c)),
            pl.BlockSpec((2 * B, 2 * B), lambda c: (0, 0)),
            pl.BlockSpec((B, 2 * B), lambda c: (0, 0)),
            pl.BlockSpec((168, 256), lambda c: (0, c)),
            pl.BlockSpec((blocks, 8, 128), lambda c: (0, 0, 0)),
        ],
        out_specs=[
            pl.BlockSpec((2 * B, 256), lambda c: (0, c)),
            pl.BlockSpec((blocks + 3, 8, 128), lambda c: (0, 0, 0)),
        ],
        out_shape=[
            pltpu.HBM((2 * B, chans), F32),
            jax.ShapeDtypeStruct((blocks + 3, 8, 128), F32),
        ],
        scratch_shapes=[
            pltpu.VMEM((3, 2, 2 * B + 8, 128), F32),
            pltpu.VMEM((3 * B, 256), BF16),
            pltpu.VMEM((3 * B, 128), F32),
        ],
        compiler_params=params(14),
        cost_estimate=cost(7 * 10**8, 4 * 10**6),
        name="mr_lower",
    )(feat, stream_in, taps, spec, forward, inverse, halo, upper)


def state_kernel(low_ref, up_ref, halo_ref, s0_ref, s1_ref, s2_ref, s3_ref, gain_ref, taps_ref,
                 q8_ref, qs_ref, normed_ref, prod_ref, state_ref, copies_ref, inv, rows_f32, *,
                 blocks):
    step = pl.program_id(0)

    @pl.when(step == 0)
    def _():
        total = s0_ref[...] + s1_ref[...] + s2_ref[...] + s3_ref[...]
        scale = lax.rsqrt(total * (1.0 / D) + EPS)
        for b in range(blocks + 1):
            spread = jnp.broadcast_to(scale[b, 0:1, :], (B, B))
            inv[b * B : (b + 1) * B, :] = jnp.transpose(spread)

    for half in range(2):
        lanes = slice(128 * half, 128 * half + 128)
        taps1, taps2 = taps_ref[1, :, lanes], taps_ref[2, :, lanes]
        gain = gain_ref[:, lanes]
        before = halo_ref[0:8, lanes].astype(F32) + halo_ref[8:16, lanes].astype(F32)
        before = (before * inv[2 * B : 2 * B + 8, :] * gain).astype(BF16)
        normed_ref[0:8, lanes] = before
        rows_f32[half, 0:8, :] = before.astype(F32)
        acc = [jnp.zeros((8, 128), F32) for _ in range(MODES)]
        q8 = [jnp.broadcast_to(q8_ref[n : n + 1, lanes], (8, 128)) for n in range(MODES)]
        for b in range(blocks):
            if b < 2:
                x = low_ref[b * B : (b + 1) * B, lanes]
                scale = inv[b * B : (b + 1) * B, :]
            else:
                x = up_ref[(b - 2) * B : (b - 1) * B, lanes]
                scale = inv[(b + 1) * B : (b + 2) * B, :]
            normed = (x * scale * gain).astype(BF16)
            start = 8 + b * B
            normed_ref[start : start + B, lanes] = normed
            rows_f32[half, start : start + B, :] = normed.astype(F32)
            keys = conv7(rows_f32.at[half], taps1, start, B)
            vals = conv7(rows_f32.at[half], taps2, start, B)
            product = (keys * vals).astype(BF16)
            prod_ref[b * B : (b + 1) * B, lanes] = product
            wide = product.astype(F32)
            for i in range(B // 8):
                part = wide[8 * i : 8 * i + 8]
                acc = [a * q + part for a, q in zip(acc, q8)]
            for n in range(MODES):
                state_ref[b, n : n + 1, lanes] = jnp.sum(
                    acc[n] * qs_ref[n, :, lanes], axis=0, keepdims=True
                )
    outgoing = state_ref[blocks - 1].astype(BF16)
    for place in range(copies_ref.shape[0]):
        copies_ref[place] = outgoing


def li_states(low, up, halo, sums, gain, taps, q8, qs, places):
    chans = low.shape[1]
    rows = low.shape[0] + up.shape[0]
    blocks = rows // B
    sum_spec = pl.BlockSpec(sums[0].shape, lambda c: (0, 0, 0))
    return pl.pallas_call(
        functools.partial(state_kernel, blocks=blocks),
        grid=(chans // 256,),
        in_specs=[
            pl.BlockSpec((2 * B, 256), lambda c: (0, c)),
            pl.BlockSpec((rows - 2 * B, 256), lambda c: (0, c)),
            pl.BlockSpec((16, 256), lambda c: (0, c)),
            sum_spec, sum_spec, sum_spec, sum_spec,
            pl.BlockSpec((1, 256), lambda c: (0, c)),
            pl.BlockSpec((3, 7, 256), lambda c: (0, 0, c)),
            pl.BlockSpec((MODES, 256), lambda c: (0, c)),
            pl.BlockSpec((MODES, 8, 256), lambda c: (0, 0, c)),
        ],
        out_specs=[
            pl.BlockSpec((8 + rows, 256), lambda c: (0, c)),
            pl.BlockSpec((rows, 256), lambda c: (0, c)),
            pl.BlockSpec((blocks, MODES, 256), lambda c: (0, 0, c)),
            pl.BlockSpec((places, MODES, 256), lambda c: (0, 0, c)),
        ],
        out_shape=[
            pltpu.HBM((8 + rows, chans), BF16),
            pltpu.HBM((rows, chans), BF16),
            jax.ShapeDtypeStruct((blocks, MODES, chans), F32),
            jax.ShapeDtypeStruct((places, MODES, chans), BF16),
        ],
        scratch_shapes=[
            pltpu.VMEM(((blocks + 1) * B, 128), F32),
            pltpu.VMEM((2, 8 + rows, 128), F32),
        ],
        compiler_params=params(20),
        cost_estimate=cost(90 * 10**6, 9 * 10**6),
        name="li_states",
    )(*in_hbm(low, up), halo, *sums, gain, taps, q8, qs)


def near_kernel(normed_ref, prod_ref, taps_ref, spec_ref, fwd_ref, inv_ref, *rest, blocks):
    near_ref, gate_ref, rows_f32 = rest[-3:]
    forward, inverse = fwd_ref[...], inv_ref[...]
    for half in range(2):
        rows_f32[half] = normed_ref[:, 128 * half : 128 * half + 128].astype(F32)
    for b in range(blocks):
        rows = slice(b * B, (b + 1) * B)
        if b % LI_GROUP == 0:
            windows = [prod_ref[i * B : (i + 1) * B, :] for i in range(b, b + LI_GROUP)]
            found = spectral(windows, forward, spec_ref[0], spec_ref[1], inverse)
        for half in range(2):
            lanes = slice(128 * half, 128 * half + 128)
            gate = conv7(rows_f32.at[half], taps_ref[0, :, lanes], 8 + b * B, B)
            gate_ref[rows, lanes] = gate.astype(BF16)
        near_ref[rows, :] = found[b % LI_GROUP].astype(BF16)


def li_near(normed, product, taps, spec, forward, inverse, part, parts, earlier=()):
    rows, chans = product.shape
    steps = chans // 256 // parts
    at = part * steps
    wide = pl.BlockSpec((rows, 256), lambda c: (0, at + c))
    return pl.pallas_call(
        functools.partial(near_kernel, blocks=rows // B),
        grid=(steps,),
        in_specs=[
            pl.BlockSpec((8 + rows, 256), lambda c: (0, at + c)),
            wide,
            pl.BlockSpec((3, 7, 256), lambda c: (0, 0, at + c)),
            pl.BlockSpec((2, B, 256), lambda c: (0, 0, at + c)),
            pl.BlockSpec((2 * B, B), lambda c: (0, 0)),
            pl.BlockSpec((B, 2 * B), lambda c: (0, 0)),
        ]
        + [pl.BlockSpec(memory_space=pl.ANY)] * len(earlier),
        out_specs=[wide, wide],
        out_shape=[pltpu.HBM((rows, chans), BF16)] * 2,
        scratch_shapes=[pltpu.VMEM((2, 8 + rows, 128), F32)],
        input_output_aliases={6 + i: i for i in range(len(earlier))},
        compiler_params=params(16),
        cost_estimate=cost(10**9 // parts, 8 * 10**6 // parts),
        name="li_near",
    )(*in_hbm(normed, product), taps, spec, forward, inverse, *in_hbm(*earlier))


def far_kernel(low_ref, up_ref, gate_ref, near_ref, state_ref, in_ref, q8_ref, q128_ref, wq_ref,
               out_ref, *, blocks):
    incoming = in_ref[...]
    for b in range(blocks):
        here = incoming if b == 0 else incoming + state_ref[b - 1]
        incoming = incoming * q128_ref[...]
        for half in range(2):
            lanes = slice(128 * half, 128 * half + 128)
            modes = [wq_ref[n, :, lanes] * here[n : n + 1, lanes] for n in range(MODES)]
            for i in range(B // 16):
                total = []
                for part in range(2):
                    level = modes
                    while len(level) > 1:
                        level = [a + c for a, c in zip(level[::2], level[1::2])]
                    total.append(level[0])
                    modes = [
                        m * jnp.broadcast_to(q8_ref[n : n + 1, lanes], (8, 128))
                        for n, m in enumerate(modes)
                    ]
                at = slice(b * B + 16 * i, b * B + 16 * i + 16)
                long = jnp.concatenate(total, axis=0) + near_ref[at, lanes].astype(F32)
                if b < 2:
                    stream = low_ref[at, lanes]
                else:
                    stream = up_ref[(b - 2) * B + 16 * i : (b - 2) * B + 16 * i + 16, lanes]
                gate = gate_ref[at, lanes].astype(F32)
                out_ref[at, lanes] = (stream + gate * long).astype(BF16)


def li_far(low, up, gate, near, states, incoming, q8, q128, wq):
    rows, chans = near.shape
    blocks = rows // B
    wide = pl.BlockSpec((rows, 256), lambda c: (0, c))
    modes = pl.BlockSpec((MODES, 256), lambda c: (0, c))
    return pl.pallas_call(
        functools.partial(far_kernel, blocks=blocks),
        grid=(chans // 256,),
        in_specs=[
            pl.BlockSpec((2 * B, 256), lambda c: (0, c)),
            pl.BlockSpec((rows - 2 * B, 256), lambda c: (0, c)),
            wide,
            wide,
            pl.BlockSpec((blocks, MODES, 256), lambda c: (0, 0, c)),
            modes,
            modes,
            modes,
            pl.BlockSpec((MODES, 8, 256), lambda c: (0, 0, c)),
        ],
        out_specs=wide,
        out_shape=jax.ShapeDtypeStruct((rows, chans), BF16),
        compiler_params=params(16),
        cost_estimate=cost(70 * 10**6, 12 * 10**6),
        name="li_far",
    )(*in_hbm(low, up, gate, near), states, incoming, q8, q128, wq)


def to_next(value):
    lines, places = lax.axis_size("line"), lax.axis_size("place")
    count = lines * places
    return lax.ppermute(value, ("line", "place"), [(i, i + 1) for i in range(count - 1)])


def to_all(value, axis):
    count = lax.axis_size(axis)
    copies = jnp.broadcast_to(value.astype(BF16)[None], (count,) + value.shape)
    return lax.all_to_all(copies, axis, 0, 0)


def weighted(parts, rates, span, upto):
    steps = upto - 1 - jnp.arange(parts.shape[0], dtype=jnp.int32)
    ages = jnp.maximum(steps, 0).astype(F32)[:, None, None] * float(span)
    terms = jnp.exp(-rates[None] * ages) * parts.astype(F32)
    return jnp.sum(jnp.where(steps[:, None, None] >= 0, terms, 0.0), axis=0)


def body(stream_in, features, mr_taps, mr_filter, norm_gain, li_taps, modal_rates, modal_weights):
    rows = stream_in.shape[0]
    feat, stream_in = in_hbm(jnp.transpose(features, (1, 0, 2)), stream_in)
    mr_t = jnp.transpose(mr_taps, (0, 2, 1))
    li_t = jnp.transpose(li_taps, (0, 2, 1))
    rates = jnp.transpose(modal_rates)
    weights = jnp.transpose(modal_weights)
    gain = norm_gain[None, :]
    fwd_np, inv_np = dft_tables()
    forward = jnp.asarray(fwd_np, BF16)
    inverse = jnp.asarray(inv_np, BF16)
    half_fwd = jnp.asarray(fwd_np[:, :B], F32)

    near_high = fwd_np[:, :B].astype(BF16)
    near_low = (fwd_np[:, :B] - near_high.astype(np.float64)).astype(BF16)
    split_fwd = jnp.asarray(np.concatenate([near_high, near_low], axis=1))
    bundle, mr_spec = mr_tail(feat, stream_in, mr_t, mr_filter, split_fwd)
    halo = to_next(bundle)
    up, up_sums = mr_upper(feat, stream_in, mr_t, mr_spec, forward, inverse[B:])
    low, own = mr_lower(feat, stream_in, mr_t, mr_spec, forward, inverse[B:], halo, up_sums)
    ways = lax.axis_size("tp")
    sums = [own] + [
        lax.ppermute(own, "tp", [(i, (i + k) % ways) for i in range(ways)]) for k in range(1, ways)
    ]

    rates, weights, own = lax.optimization_barrier((rates, weights, own))
    scaled = weights * jnp.sqrt(1.0 - jnp.exp(-2.0 * rates))
    lags = jnp.arange(B, dtype=F32)
    coarse = jnp.exp(-rates[None] * (8.0 * lags)[: B // 8, None, None])
    fine = scaled[None] * jnp.exp(-rates[None] * lags[:8, None, None])
    coarse, fine = lax.optimization_barrier((coarse, fine))
    near_taps = jnp.sum(coarse[:, None] * fine[None], axis=2).reshape(B, -1)
    li_spec = jnp.dot(half_fwd, near_taps, precision=HIGH).reshape(2, B, -1)
    within = jnp.arange(8, dtype=F32)[None, :, None]
    q8 = jnp.exp(-8.0 * rates)
    q128 = jnp.exp(-float(B) * rates)
    qs = jnp.exp(-rates[:, None, :] * (7.0 - within))
    wq = scaled[:, None, :] * jnp.exp(-rates[:, None, :] * (within + 1.0))
    gain, li_spec, wq, q128 = lax.optimization_barrier((gain, li_spec, wq, q128))

    near_args = (li_t, li_spec, forward[:, :B], inverse[:B])
    place, line = lax.axis_index("place"), lax.axis_index("line")
    places = lax.axis_size("place")
    normed, product, states, copies = li_states(
        low, up, halo[152:168], sums, gain, li_t, q8, qs, places
    )
    with jax.named_scope("scan_places"):
        parts = lax.all_to_all(copies, "place", 0, 0)
    first = li_near(normed, product, *near_args, 0, 2)
    with jax.named_scope("scan_places"):
        parts, first = lax.optimization_barrier((parts, first))
        whole = weighted(parts, rates, rows, places)
        prefix = weighted(parts, rates, rows, place)
    with jax.named_scope("scan_lines"):
        parts = to_all(whole, "line")
    normed, whole = lax.optimization_barrier((normed, whole))
    near, gate = li_near(normed, product, *near_args, 1, 2, first)
    with jax.named_scope("scan_lines"):
        parts, near, gate = lax.optimization_barrier((parts, near, gate))
        before = weighted(parts, rates, rows * places, line)
        incoming = prefix + before * jnp.exp(-rates * (rows * place.astype(F32)))
    return li_far(low, up, gate, near, states, incoming, q8, q128, wq)


def solution(mesh):
    ctx, tp = mesh.devices.shape
    places = 8 if ctx % 8 == 0 else ctx
    split = jax.sharding.Mesh(
        mesh.devices.reshape(ctx // places, places, tp), ("line", "place", "tp")
    )
    seq = ("line", "place")
    in_specs = (
        P(seq, "tp"),
        P(seq, None, "tp"),
        P(None, "tp", None),
        P("tp", None),
        P("tp"),
        P(None, "tp", None),
        P("tp", None),
        P("tp", None),
    )
    return jax.shard_map(
        body, mesh=split, in_specs=in_specs, out_specs=P(seq, "tp"), check_vma=False
    )
```

```python
import functools

import jax
import jax.numpy as jnp
import numpy as np
from jax import lax
from jax.experimental import pallas as pl
from jax.experimental.pallas import tpu as pltpu
from jax.sharding import PartitionSpec as P

D = 4096
EPS = 1e-06
MODES = 16
B = 128
LI_GROUP = 2
HIGH = lax.Precision.HIGHEST
F32 = jnp.float32
BF16 = jnp.bfloat16


def dft_tables():
    j = np.arange(2 * B)
    k = np.arange(B)
    angle = np.pi * (2 * k[:, None] + 1) * j[None, :] / (2 * B)
    cos, sin = np.cos(angle), np.sin(angle)
    forward = np.concatenate([cos, -sin], axis=0)
    inverse = np.concatenate([cos.T, -sin.T], axis=1) / B
    return forward, inverse


def params(mib):
    return pltpu.CompilerParams(vmem_limit_bytes=mib * 2**20)


def in_hbm(*values):
    return [pltpu.with_memory_space_constraint(value, pltpu.HBM) for value in values]


def cost(flops, bytes_accessed):
    return pl.CostEstimate(flops=flops, bytes_accessed=bytes_accessed, transcendentals=0)


def conv7(rows_ref, taps, start, count):
    total = taps[0:1] * rows_ref[pl.ds(start, count), :]
    for tap in range(1, 7):
        total = total + taps[tap : tap + 1] * rows_ref[pl.ds(start - tap, count), :]
    return total


def tail_kernel(feat_ref, stream_ref, taps_ref, filt_ref, fwd_ref, out_ref, spec_ref, feat, prod, filt):
    n_in, n_prod = 160, 144
    first = 256 - n_in
    turned = jnp.transpose(filt_ref[...].astype(F32))
    filt[...] = turned
    twice = jnp.concatenate([turned, turned], axis=0).astype(BF16)
    spec = jnp.dot(fwd_ref[...], twice, preferred_element_type=F32)
    spec_ref[0] = spec[:B]
    spec_ref[1] = spec[B:]
    for half in range(2):
        lanes = slice(128 * half, 128 * half + 128)
        for s in range(3):
            feat[s] = feat_ref[s, first:256, lanes].astype(F32)
        keys = conv7(feat.at[1], taps_ref[1, :, lanes], 16, n_prod)
        vals = conv7(feat.at[2], taps_ref[2, :, lanes], 16, n_prod)
        product = (keys * vals).astype(BF16)
        prod[...] = product.astype(F32)
        medium = jnp.zeros((8, 128), F32)
        for lag in range(128):
            medium = medium + filt[lag : lag + 1, lanes] * prod[pl.ds(136 - lag, 8), :]
        gate = conv7(feat.at[0], taps_ref[0, :, lanes], n_in - 8, 8)
        stream = stream_ref[8:16, lanes].astype(F32) + gate * medium
        high = stream.astype(BF16)
        out_ref[0:128, lanes] = product[16:144]
        for s in range(3):
            out_ref[128 + 8 * s : 136 + 8 * s, lanes] = feat_ref[s, 248:256, lanes]
        out_ref[152:160, lanes] = high
        out_ref[160:168, lanes] = (stream - high.astype(F32)).astype(BF16)


def mr_tail(feat, stream_in, taps, filt, forward):
    rows, chans = stream_in.shape
    last = rows // 256 - 1
    end = rows // 16 - 1
    return pl.pallas_call(
        tail_kernel,
        grid=(chans // 256,),
        in_specs=[
            pl.BlockSpec((3, 256, 256), lambda c: (0, last, c)),
            pl.BlockSpec((16, 256), lambda c: (end, c)),
            pl.BlockSpec((3, 7, 256), lambda c: (0, 0, c)),
            pl.BlockSpec((256, 128), lambda c: (c, 0)),
            pl.BlockSpec((2 * B, 2 * B), lambda c: (0, 0)),
        ],
        out_specs=[
            pl.BlockSpec((168, 256), lambda c: (0, c)),
            pl.BlockSpec((2, B, 256), lambda c: (0, 0, c)),
        ],
        out_shape=[
            jax.ShapeDtypeStruct((168, chans), BF16),
            jax.ShapeDtypeStruct((2, B, chans), F32),
        ],
        scratch_shapes=[
            pltpu.VMEM((3, 160, 128), F32),
            pltpu.VMEM((144, 128), F32),
            pltpu.VMEM((128, 256), F32),
        ],
        compiler_params=params(12),
        cost_estimate=cost(20 * 10**6, 2 * 10**6),
        name="mr_tail",
    )(feat, stream_in, *in_hbm(taps, filt, forward))


def spectral(windows, forward, real, imag, inverse):
    count, width = len(windows), windows[0].shape[1]
    spec = jnp.dot(forward, jnp.concatenate(windows, axis=1), preferred_element_type=F32)
    xr, xi = spec[:B], spec[B:]
    real = jnp.concatenate([real] * count, axis=1)
    imag = jnp.concatenate([imag] * count, axis=1)
    out = jnp.concatenate([xr * real - xi * imag, xr * imag + xi * real], axis=0)
    found = jnp.dot(inverse, out.astype(BF16), preferred_element_type=F32)
    return [found[:, width * i : width * (i + 1)] for i in range(count)]


def put_row_sums(squares, count):
    ones = jnp.ones((8, 128), F32)
    return lax.dot_general(
        ones, squares, (((1,), (1,)), ((), ())), precision=HIGH, preferred_element_type=F32
    )


def mr_rows(feat_ref, stream_ref, taps_ref, spec_ref, fwd_ref, inv_ref, out_ref, feat, prod, sums,
            first, blocks, ready=()):
    forward, inverse = fwd_ref[...], inv_ref[...]
    per = 3 if blocks % 3 == 0 else 2

    def make_product(b):
        start = 8 + (b - 1) * B if first == 0 else 8 + b * B
        for half in range(2):
            lanes = slice(128 * half, 128 * half + 128)
            keys = conv7(feat.at[1, half], taps_ref[1, :, lanes], start, B)
            vals = conv7(feat.at[2, half], taps_ref[2, :, lanes], start, B)
            prod[b * B : (b + 1) * B, lanes] = (keys * vals).astype(BF16)

    for b in range(per + 1):
        if b not in ready:
            make_product(b)
    for group in range(0, blocks, per):
        windows = [prod[i * B : (i + 2) * B, :] for i in range(group, group + per)]
        found = spectral(windows, forward, spec_ref[0], spec_ref[1], inverse)
        for b in range(group + per + 1, min(group + 2 * per, blocks) + 1):
            make_product(b)
        for b in range(group, group + per):
            rows = slice(b * B, (b + 1) * B)
            start = 8 + b * B if first == 0 else 8 + (b + 1) * B
            for half in range(2):
                lanes = slice(128 * half, 128 * half + 128)
                gate = conv7(feat.at[0, half], taps_ref[0, :, lanes], start, B)
                stream = stream_ref[first + b * B : first + (b + 1) * B, lanes].astype(F32)
                stream = stream + gate * found[b - group][:, lanes]
                out_ref[rows, lanes] = stream
                sums[rows, :] += stream * stream


def upper_kernel(feat_ref, stream_ref, taps_ref, spec_ref, fwd_ref, inv_ref, out_ref, sum_ref,
                 middle_ref, feat, prod, sums, *, blocks):
    step = pl.program_id(0)

    @pl.when(step == 0)
    def _():
        sums[...] = jnp.zeros_like(sums)

    for s in range(3):
        for half in range(2):
            feat[s, half] = feat_ref[s, 120:, 128 * half : 128 * half + 128].astype(F32)
    mr_rows(feat_ref, stream_ref, taps_ref, spec_ref, fwd_ref, inv_ref, out_ref, feat, prod, sums,
            2 * B, blocks)
    middle_ref[...] = prod[0:B, :]

    @pl.when(step == pl.num_programs(0) - 1)
    def _():
        for b in range(blocks):
            sum_ref[b] = put_row_sums(sums[b * B : (b + 1) * B, :], B)


def mr_upper(feat, stream_in, taps, spec, forward, inverse):
    rows, chans = stream_in.shape
    blocks = rows // B - 2
    return pl.pallas_call(
        functools.partial(upper_kernel, blocks=blocks),
        grid=(chans // 256,),
        in_specs=[
            pl.BlockSpec((3, rows, 256), lambda c: (0, 0, c)),
            pl.BlockSpec((rows, 256), lambda c: (0, c)),
            pl.BlockSpec((3, 7, 256), lambda c: (0, 0, c)),
            pl.BlockSpec((2, B, 256), lambda c: (0, 0, c)),
            pl.BlockSpec((2 * B, 2 * B), lambda c: (0, 0)),
            pl.BlockSpec((B, 2 * B), lambda c: (0, 0)),
        ],
        out_specs=[
            pl.BlockSpec((blocks * B, 256), lambda c: (0, c)),
            pl.BlockSpec((blocks, 8, 128), lambda c: (0, 0, 0)),
            pl.BlockSpec((B, 256), lambda c: (0, c)),
        ],
        out_shape=[
            pltpu.HBM((blocks * B, chans), F32),
            jax.ShapeDtypeStruct((blocks, 8, 128), F32),
            pltpu.HBM((B, chans), BF16),
        ],
        scratch_shapes=[
            pltpu.VMEM((3, 2, rows - 120, 128), F32),
            pltpu.VMEM(((blocks + 1) * B, 256), BF16),
            pltpu.VMEM((blocks * B, 128), F32),
        ],
        compiler_params=params(20),
        cost_estimate=cost(2 * 10**9, 14 * 10**6),
        name="mr_upper",
    )(feat, stream_in, taps, spec, forward, inverse)


def lower_kernel(feat_ref, stream_ref, taps_ref, spec_ref, fwd_ref, inv_ref, halo_ref, upper_ref,
                 middle_ref, out_ref, sum_ref, feat, prod, sums, *, blocks):
    step = pl.program_id(0)

    @pl.when(step == 0)
    def _():
        sums[...] = jnp.zeros_like(sums)

    for half in range(2):
        lanes = slice(128 * half, 128 * half + 128)
        for s in range(3):
            feat[s, half, 0:8] = halo_ref[128 + 8 * s : 136 + 8 * s, lanes].astype(F32)
            feat[s, half, 8:] = feat_ref[s, :, lanes].astype(F32)
        before = halo_ref[152:160, lanes].astype(F32) + halo_ref[160:168, lanes].astype(F32)
        sums[2 * B : 2 * B + 8, :] += before * before
    prod[0:B, :] = halo_ref[0:B, :]
    prod[2 * B : 3 * B, :] = middle_ref[...]
    mr_rows(feat_ref, stream_ref, taps_ref, spec_ref, fwd_ref, inv_ref, out_ref, feat, prod, sums,
            0, 2, ready=(0, 2))

    @pl.when(step == pl.num_programs(0) - 1)
    def _():
        for b in range(3):
            sum_ref[b] = put_row_sums(sums[b * B : (b + 1) * B, :], B)
        sum_ref[3:] = upper_ref[...]


def mr_lower(feat, stream_in, taps, spec, forward, inverse, halo, upper, middle):
    rows, chans = stream_in.shape
    blocks = upper.shape[0]
    return pl.pallas_call(
        functools.partial(lower_kernel, blocks=blocks),
        grid=(chans // 256,),
        in_specs=[
            pl.BlockSpec((3, 2 * B, 256), lambda c: (0, 0, c)),
            pl.BlockSpec((2 * B, 256), lambda c: (0, c)),
            pl.BlockSpec((3, 7, 256), lambda c: (0, 0, c)),
            pl.BlockSpec((2, B, 256), lambda c: (0, 0, c)),
            pl.BlockSpec((2 * B, 2 * B), lambda c: (0, 0)),
            pl.BlockSpec((B, 2 * B), lambda c: (0, 0)),
            pl.BlockSpec((168, 256), lambda c: (0, c)),
            pl.BlockSpec((blocks, 8, 128), lambda c: (0, 0, 0)),
            pl.BlockSpec((B, 256), lambda c: (0, c)),
        ],
        out_specs=[
            pl.BlockSpec((2 * B, 256), lambda c: (0, c)),
            pl.BlockSpec((blocks + 3, 8, 128), lambda c: (0, 0, 0)),
        ],
        out_shape=[
            pltpu.HBM((2 * B, chans), F32),
            jax.ShapeDtypeStruct((blocks + 3, 8, 128), F32),
        ],
        scratch_shapes=[
            pltpu.VMEM((3, 2, 2 * B + 8, 128), F32),
            pltpu.VMEM((3 * B, 256), BF16),
            pltpu.VMEM((3 * B, 128), F32),
        ],
        compiler_params=params(14),
        cost_estimate=cost(7 * 10**8, 4 * 10**6),
        name="mr_lower",
    )(feat, stream_in, taps, spec, forward, inverse, halo, upper, *in_hbm(middle))


def state_kernel(low_ref, up_ref, halo_ref, s0_ref, s1_ref, s2_ref, s3_ref, gain_ref, taps_ref,
                 q8_ref, qs_ref, normed_ref, prod_ref, state_ref, copies_ref, inv, rows_f32, *,
                 blocks):
    step = pl.program_id(0)

    @pl.when(step == 0)
    def _():
        total = s0_ref[...] + s1_ref[...] + s2_ref[...] + s3_ref[...]
        scale = lax.rsqrt(total * (1.0 / D) + EPS)
        for b in range(blocks + 1):
            spread = jnp.broadcast_to(scale[b, 0:1, :], (B, B))
            inv[b * B : (b + 1) * B, :] = jnp.transpose(spread)

    for half in range(2):
        lanes = slice(128 * half, 128 * half + 128)
        taps1, taps2 = taps_ref[1, :, lanes], taps_ref[2, :, lanes]
        gain = gain_ref[:, lanes]
        before = halo_ref[0:8, lanes].astype(F32) + halo_ref[8:16, lanes].astype(F32)
        before = (before * inv[2 * B : 2 * B + 8, :] * gain).astype(BF16)
        normed_ref[0:8, lanes] = before
        rows_f32[half, 0:8, :] = before.astype(F32)
        acc = [jnp.zeros((8, 128), F32) for _ in range(MODES)]
        q8 = [jnp.broadcast_to(q8_ref[n : n + 1, lanes], (8, 128)) for n in range(MODES)]
        for b in range(blocks):
            if b < 2:
                x = low_ref[b * B : (b + 1) * B, lanes]
                scale = inv[b * B : (b + 1) * B, :]
            else:
                x = up_ref[(b - 2) * B : (b - 1) * B, lanes]
                scale = inv[(b + 1) * B : (b + 2) * B, :]
            normed = (x * scale * gain).astype(BF16)
            start = 8 + b * B
            normed_ref[start : start + B, lanes] = normed
            rows_f32[half, start : start + B, :] = normed.astype(F32)
            keys = conv7(rows_f32.at[half], taps1, start, B)
            vals = conv7(rows_f32.at[half], taps2, start, B)
            product = (keys * vals).astype(BF16)
            prod_ref[b * B : (b + 1) * B, lanes] = product
            wide = product.astype(F32)
            for i in range(B // 8):
                part = wide[8 * i : 8 * i + 8]
                acc = [a * q + part for a, q in zip(acc, q8)]
            for n in range(MODES):
                state_ref[b, n : n + 1, lanes] = jnp.sum(
                    acc[n] * qs_ref[n, :, lanes], axis=0, keepdims=True
                )
    outgoing = state_ref[blocks - 1].astype(BF16)
    for place in range(copies_ref.shape[0]):
        copies_ref[place] = outgoing


def li_states(low, up, halo, sums, gain, taps, q8, qs, places):
    chans = low.shape[1]
    rows = low.shape[0] + up.shape[0]
    blocks = rows // B
    sum_spec = pl.BlockSpec(sums[0].shape, lambda c: (0, 0, 0))
    return pl.pallas_call(
        functools.partial(state_kernel, blocks=blocks),
        grid=(chans // 256,),
        in_specs=[
            pl.BlockSpec((2 * B, 256), lambda c: (0, c)),
            pl.BlockSpec((rows - 2 * B, 256), lambda c: (0, c)),
            pl.BlockSpec((16, 256), lambda c: (0, c)),
            sum_spec, sum_spec, sum_spec, sum_spec,
            pl.BlockSpec((1, 256), lambda c: (0, c)),
            pl.BlockSpec((3, 7, 256), lambda c: (0, 0, c)),
            pl.BlockSpec((MODES, 256), lambda c: (0, c)),
            pl.BlockSpec((MODES, 8, 256), lambda c: (0, 0, c)),
        ],
        out_specs=[
            pl.BlockSpec((8 + rows, 256), lambda c: (0, c)),
            pl.BlockSpec((rows, 256), lambda c: (0, c)),
            pl.BlockSpec((blocks, MODES, 256), lambda c: (0, 0, c)),
            pl.BlockSpec((places, MODES, 256), lambda c: (0, 0, c)),
        ],
        out_shape=[
            pltpu.HBM((8 + rows, chans), BF16),
            pltpu.HBM((rows, chans), BF16),
            jax.ShapeDtypeStruct((blocks, MODES, chans), F32),
            jax.ShapeDtypeStruct((places, MODES, chans), BF16),
        ],
        scratch_shapes=[
            pltpu.VMEM(((blocks + 1) * B, 128), F32),
            pltpu.VMEM((2, 8 + rows, 128), F32),
        ],
        compiler_params=params(20),
        cost_estimate=cost(90 * 10**6, 9 * 10**6),
        name="li_states",
    )(*in_hbm(low, up), halo, *sums, gain, taps, q8, qs)


def near_kernel(normed_ref, prod_ref, taps_ref, spec_ref, fwd_ref, inv_ref, *rest, blocks):
    near_ref, gate_ref, rows_f32 = rest[-3:]
    forward, inverse = fwd_ref[...], inv_ref[...]
    for half in range(2):
        rows_f32[half] = normed_ref[:, 128 * half : 128 * half + 128].astype(F32)
    for b in range(blocks):
        rows = slice(b * B, (b + 1) * B)
        if b % LI_GROUP == 0:
            windows = [prod_ref[i * B : (i + 1) * B, :] for i in range(b, b + LI_GROUP)]
            found = spectral(windows, forward, spec_ref[0], spec_ref[1], inverse)
        for half in range(2):
            lanes = slice(128 * half, 128 * half + 128)
            gate = conv7(rows_f32.at[half], taps_ref[0, :, lanes], 8 + b * B, B)
            gate_ref[rows, lanes] = gate.astype(BF16)
        near_ref[rows, :] = found[b % LI_GROUP].astype(BF16)


def li_near(normed, product, taps, spec, forward, inverse, part, parts, earlier=()):
    rows, chans = product.shape
    steps = chans // 256 // parts
    at = part * steps
    wide = pl.BlockSpec((rows, 256), lambda c: (0, at + c))
    return pl.pallas_call(
        functools.partial(near_kernel, blocks=rows // B),
        grid=(steps,),
        in_specs=[
            pl.BlockSpec((8 + rows, 256), lambda c: (0, at + c)),
            wide,
            pl.BlockSpec((3, 7, 256), lambda c: (0, 0, at + c)),
            pl.BlockSpec((2, B, 256), lambda c: (0, 0, at + c)),
            pl.BlockSpec((2 * B, B), lambda c: (0, 0)),
            pl.BlockSpec((B, 2 * B), lambda c: (0, 0)),
        ]
        + [pl.BlockSpec(memory_space=pl.ANY)] * len(earlier),
        out_specs=[wide, wide],
        out_shape=[pltpu.HBM((rows, chans), BF16)] * 2,
        scratch_shapes=[pltpu.VMEM((2, 8 + rows, 128), F32)],
        input_output_aliases={6 + i: i for i in range(len(earlier))},
        compiler_params=params(16),
        cost_estimate=cost(10**9 // parts, 8 * 10**6 // parts),
        name="li_near",
    )(*in_hbm(normed, product), taps, spec, forward, inverse, *in_hbm(*earlier))


def far_kernel(low_ref, up_ref, gate_ref, near_ref, state_ref, in_ref, q8_ref, q128_ref, wq_ref,
               out_ref, *, blocks):
    incoming = in_ref[...]
    for b in range(blocks):
        here = incoming if b == 0 else incoming + state_ref[b - 1]
        incoming = incoming * q128_ref[...]
        for half in range(2):
            lanes = slice(128 * half, 128 * half + 128)
            modes = [wq_ref[n, :, lanes] * here[n : n + 1, lanes] for n in range(MODES)]
            for i in range(B // 16):
                total = []
                for part in range(2):
                    level = modes
                    while len(level) > 1:
                        level = [a + c for a, c in zip(level[::2], level[1::2])]
                    total.append(level[0])
                    modes = [
                        m * jnp.broadcast_to(q8_ref[n : n + 1, lanes], (8, 128))
                        for n, m in enumerate(modes)
                    ]
                at = slice(b * B + 16 * i, b * B + 16 * i + 16)
                long = jnp.concatenate(total, axis=0) + near_ref[at, lanes].astype(F32)
                if b < 2:
                    stream = low_ref[at, lanes]
                else:
                    stream = up_ref[(b - 2) * B + 16 * i : (b - 2) * B + 16 * i + 16, lanes]
                gate = gate_ref[at, lanes].astype(F32)
                out_ref[at, lanes] = (stream + gate * long).astype(BF16)


def li_far(low, up, gate, near, states, incoming, q8, q128, wq):
    rows, chans = near.shape
    blocks = rows // B
    wide = pl.BlockSpec((rows, 256), lambda c: (0, c))
    modes = pl.BlockSpec((MODES, 256), lambda c: (0, c))
    return pl.pallas_call(
        functools.partial(far_kernel, blocks=blocks),
        grid=(chans // 256,),
        in_specs=[
            pl.BlockSpec((2 * B, 256), lambda c: (0, c)),
            pl.BlockSpec((rows - 2 * B, 256), lambda c: (0, c)),
            wide,
            wide,
            pl.BlockSpec((blocks, MODES, 256), lambda c: (0, 0, c)),
            modes,
            modes,
            modes,
            pl.BlockSpec((MODES, 8, 256), lambda c: (0, 0, c)),
        ],
        out_specs=wide,
        out_shape=jax.ShapeDtypeStruct((rows, chans), BF16),
        compiler_params=params(16),
        cost_estimate=cost(70 * 10**6, 12 * 10**6),
        name="li_far",
    )(*in_hbm(low, up, gate, near), states, incoming, q8, q128, wq)


def to_next(value):
    lines, places = lax.axis_size("line"), lax.axis_size("place")
    count = lines * places
    return lax.ppermute(value, ("line", "place"), [(i, i + 1) for i in range(count - 1)])


def to_all(value, axis):
    count = lax.axis_size(axis)
    copies = jnp.broadcast_to(value.astype(BF16)[None], (count,) + value.shape)
    return lax.all_to_all(copies, axis, 0, 0)


def weighted(parts, rates, span, upto):
    steps = upto - 1 - jnp.arange(parts.shape[0], dtype=jnp.int32)
    ages = jnp.maximum(steps, 0).astype(F32)[:, None, None] * float(span)
    terms = jnp.exp(-rates[None] * ages) * parts.astype(F32)
    return jnp.sum(jnp.where(steps[:, None, None] >= 0, terms, 0.0), axis=0)


def body(stream_in, features, mr_taps, mr_filter, norm_gain, li_taps, modal_rates, modal_weights):
    rows = stream_in.shape[0]
    feat, stream_in = in_hbm(jnp.transpose(features, (1, 0, 2)), stream_in)
    mr_t = jnp.transpose(mr_taps, (0, 2, 1))
    li_t = jnp.transpose(li_taps, (0, 2, 1))
    rates = jnp.transpose(modal_rates)
    weights = jnp.transpose(modal_weights)
    gain = norm_gain[None, :]
    fwd_np, inv_np = dft_tables()
    forward = jnp.asarray(fwd_np, BF16)
    inverse = jnp.asarray(inv_np, BF16)
    half_fwd = jnp.asarray(fwd_np[:, :B], F32)

    near_high = fwd_np[:, :B].astype(BF16)
    near_low = (fwd_np[:, :B] - near_high.astype(np.float64)).astype(BF16)
    split_fwd = jnp.asarray(np.concatenate([near_high, near_low], axis=1))
    bundle, mr_spec = mr_tail(feat, stream_in, mr_t, mr_filter, split_fwd)
    halo = to_next(bundle)
    up, up_sums, middle = mr_upper(feat, stream_in, mr_t, mr_spec, forward, inverse[B:])
    low, own = mr_lower(feat, stream_in, mr_t, mr_spec, forward, inverse[B:], halo, up_sums, middle)
    ways = lax.axis_size("tp")
    sums = [own] + [
        lax.ppermute(own, "tp", [(i, (i + k) % ways) for i in range(ways)]) for k in range(1, ways)
    ]

    rates, weights, own = lax.optimization_barrier((rates, weights, own))
    scaled = weights * jnp.sqrt(1.0 - jnp.exp(-2.0 * rates))
    lags = jnp.arange(B, dtype=F32)
    coarse = jnp.exp(-rates[None] * (8.0 * lags)[: B // 8, None, None])
    fine = scaled[None] * jnp.exp(-rates[None] * lags[:8, None, None])
    coarse, fine = lax.optimization_barrier((coarse, fine))
    near_taps = jnp.sum(coarse[:, None] * fine[None], axis=2).reshape(B, -1)
    li_spec = jnp.dot(half_fwd, near_taps, precision=lax.Precision.HIGH).reshape(2, B, -1)
    within = jnp.arange(8, dtype=F32)[None, :, None]
    q8 = jnp.exp(-8.0 * rates)
    q128 = jnp.exp(-float(B) * rates)
    qs = jnp.exp(-rates[:, None, :] * (7.0 - within))
    wq = scaled[:, None, :] * jnp.exp(-rates[:, None, :] * (within + 1.0))
    gain, li_spec, wq, q128 = lax.optimization_barrier((gain, li_spec, wq, q128))

    near_args = (li_t, li_spec, forward[:, :B], inverse[:B])
    place, line = lax.axis_index("place"), lax.axis_index("line")
    places = lax.axis_size("place")
    normed, product, states, copies = li_states(
        low, up, halo[152:168], sums, gain, li_t, q8, qs, places
    )
    with jax.named_scope("scan_places"):
        parts = lax.all_to_all(copies, "place", 0, 0)
    first = li_near(normed, product, *near_args, 0, 2)
    with jax.named_scope("scan_places"):
        parts, first = lax.optimization_barrier((parts, first))
        whole = weighted(parts, rates, rows, places)
        prefix = weighted(parts, rates, rows, place)
    with jax.named_scope("scan_lines"):
        parts = to_all(whole, "line")
    normed, whole = lax.optimization_barrier((normed, whole))
    near, gate = li_near(normed, product, *near_args, 1, 2, first)
    with jax.named_scope("scan_lines"):
        parts, near, gate = lax.optimization_barrier((parts, near, gate))
        before = weighted(parts, rates, rows * places, line)
        incoming = prefix + before * jnp.exp(-rates * (rows * place.astype(F32)))
    return li_far(low, up, gate, near, states, incoming, q8, q128, wq)


def solution(mesh):
    ctx, tp = mesh.devices.shape
    places = 8 if ctx % 8 == 0 else ctx
    split = jax.sharding.Mesh(
        mesh.devices.reshape(ctx // places, places, tp), ("line", "place", "tp")
    )
    seq = ("line", "place")
    in_specs = (
        P(seq, "tp"),
        P(seq, None, "tp"),
        P(None, "tp", None),
        P("tp", None),
        P("tp"),
        P(None, "tp", None),
        P("tp", None),
        P("tp", None),
    )
    return jax.shard_map(
        body, mesh=split, in_specs=in_specs, out_specs=P(seq, "tp"), check_vma=False
    )
```

```python
import functools

import jax
import jax.numpy as jnp
import numpy as np
from jax import lax
from jax.experimental import pallas as pl
from jax.experimental.pallas import tpu as pltpu
from jax.sharding import PartitionSpec as P

D = 4096
EPS = 1e-06
MODES = 16
B = 128
LI_GROUP = 2
HIGH = lax.Precision.HIGHEST
F32 = jnp.float32
BF16 = jnp.bfloat16


def dft_tables():
    j = np.arange(2 * B)
    k = np.arange(B)
    angle = np.pi * (2 * k[:, None] + 1) * j[None, :] / (2 * B)
    cos, sin = np.cos(angle), np.sin(angle)
    forward = np.concatenate([cos, -sin], axis=0)
    inverse = np.concatenate([cos.T, -sin.T], axis=1) / B
    return forward, inverse


def params(mib):
    return pltpu.CompilerParams(vmem_limit_bytes=mib * 2**20)


def in_hbm(*values):
    return [pltpu.with_memory_space_constraint(value, pltpu.HBM) for value in values]


def cost(flops, bytes_accessed):
    return pl.CostEstimate(flops=flops, bytes_accessed=bytes_accessed, transcendentals=0)


def conv7(rows_ref, taps, start, count):
    total = taps[0:1] * rows_ref[pl.ds(start, count), :]
    for tap in range(1, 7):
        total = total + taps[tap : tap + 1] * rows_ref[pl.ds(start - tap, count), :]
    return total


def tail_kernel(feat_ref, stream_ref, taps_ref, filt_ref, fwd_ref, out_ref, spec_ref, feat, prod, filt):
    n_in, n_prod = 160, 144
    first = 256 - n_in
    turned = jnp.transpose(filt_ref[...].astype(F32))
    filt[...] = turned
    twice = jnp.concatenate([turned, turned], axis=0).astype(BF16)
    spec = jnp.dot(fwd_ref[...], twice, preferred_element_type=F32)
    spec_ref[0] = spec[:B]
    spec_ref[1] = spec[B:]
    for half in range(2):
        lanes = slice(128 * half, 128 * half + 128)
        for s in range(3):
            feat[s] = feat_ref[s, first:256, lanes].astype(F32)
        keys = conv7(feat.at[1], taps_ref[1, :, lanes], 16, n_prod)
        vals = conv7(feat.at[2], taps_ref[2, :, lanes], 16, n_prod)
        product = (keys * vals).astype(BF16)
        prod[...] = product.astype(F32)
        medium = jnp.zeros((8, 128), F32)
        for lag in range(128):
            medium = medium + filt[lag : lag + 1, lanes] * prod[pl.ds(136 - lag, 8), :]
        gate = conv7(feat.at[0], taps_ref[0, :, lanes], n_in - 8, 8)
        stream = stream_ref[8:16, lanes].astype(F32) + gate * medium
        high = stream.astype(BF16)
        out_ref[0:128, lanes] = product[16:144]
        for s in range(3):
            out_ref[128 + 8 * s : 136 + 8 * s, lanes] = feat_ref[s, 248:256, lanes]
        out_ref[152:160, lanes] = high
        out_ref[160:168, lanes] = (stream - high.astype(F32)).astype(BF16)


def mr_tail(feat, stream_in, taps, filt, forward):
    rows, chans = stream_in.shape
    last = rows // 256 - 1
    end = rows // 16 - 1
    return pl.pallas_call(
        tail_kernel,
        grid=(chans // 256,),
        in_specs=[
            pl.BlockSpec((3, 256, 256), lambda c: (0, last, c)),
            pl.BlockSpec((16, 256), lambda c: (end, c)),
            pl.BlockSpec((3, 7, 256), lambda c: (0, 0, c)),
            pl.BlockSpec((256, 128), lambda c: (c, 0)),
            pl.BlockSpec((2 * B, 2 * B), lambda c: (0, 0)),
        ],
        out_specs=[
            pl.BlockSpec((168, 256), lambda c: (0, c)),
            pl.BlockSpec((2, B, 256), lambda c: (0, 0, c)),
        ],
        out_shape=[
            jax.ShapeDtypeStruct((168, chans), BF16),
            jax.ShapeDtypeStruct((2, B, chans), F32),
        ],
        scratch_shapes=[
            pltpu.VMEM((3, 160, 128), F32),
            pltpu.VMEM((144, 128), F32),
            pltpu.VMEM((128, 256), F32),
        ],
        compiler_params=params(12),
        cost_estimate=cost(20 * 10**6, 2 * 10**6),
        name="mr_tail",
    )(feat, stream_in, *in_hbm(taps, filt, forward))


def spectral(windows, forward, real, imag, inverse):
    count, width = len(windows), windows[0].shape[1]
    spec = jnp.dot(forward, jnp.concatenate(windows, axis=1), preferred_element_type=F32)
    xr, xi = spec[:B], spec[B:]
    real = jnp.concatenate([real] * count, axis=1)
    imag = jnp.concatenate([imag] * count, axis=1)
    out = jnp.concatenate([xr * real - xi * imag, xr * imag + xi * real], axis=0)
    found = jnp.dot(inverse, out.astype(BF16), preferred_element_type=F32)
    return [found[:, width * i : width * (i + 1)] for i in range(count)]


def put_row_sums(squares, count):
    ones = jnp.ones((8, 128), F32)
    return lax.dot_general(
        ones, squares, (((1,), (1,)), ((), ())), precision=HIGH, preferred_element_type=F32
    )


def mr_rows(feat_ref, stream_ref, taps_ref, spec_ref, fwd_ref, inv_ref, out_ref, feat, prod, sums,
            first, blocks, ready=()):
    forward, inverse = fwd_ref[...], inv_ref[...]
    per = 3 if blocks % 3 == 0 else 2

    def make_product(b):
        start = 8 + (b - 1) * B if first == 0 else 8 + b * B
        for half in range(2):
            lanes = slice(128 * half, 128 * half + 128)
            keys = conv7(feat.at[1, half], taps_ref[1, :, lanes], start, B)
            vals = conv7(feat.at[2, half], taps_ref[2, :, lanes], start, B)
            prod[b * B : (b + 1) * B, lanes] = (keys * vals).astype(BF16)

    for b in range(per + 1):
        if b not in ready:
            make_product(b)
    for group in range(0, blocks, per):
        windows = [prod[i * B : (i + 2) * B, :] for i in range(group, group + per)]
        found = spectral(windows, forward, spec_ref[0], spec_ref[1], inverse)
        for b in range(group + per + 1, min(group + 2 * per, blocks) + 1):
            make_product(b)
        for b in range(group, group + per):
            rows = slice(b * B, (b + 1) * B)
            start = 8 + b * B if first == 0 else 8 + (b + 1) * B
            for half in range(2):
                lanes = slice(128 * half, 128 * half + 128)
                gate = conv7(feat.at[0, half], taps_ref[0, :, lanes], start, B)
                stream = stream_ref[first + b * B : first + (b + 1) * B, lanes].astype(F32)
                stream = stream + gate * found[b - group][:, lanes]
                out_ref[rows, lanes] = stream
                sums[rows, :] += stream * stream


def upper_kernel(feat_ref, stream_ref, taps_ref, spec_ref, fwd_ref, inv_ref, out_ref, sum_ref,
                 middle_ref, feat, prod, sums, *, blocks):
    step = pl.program_id(0)

    @pl.when(step == 0)
    def _():
        sums[...] = jnp.zeros_like(sums)

    for s in range(3):
        for half in range(2):
            feat[s, half] = feat_ref[s, 120:, 128 * half : 128 * half + 128].astype(F32)
    mr_rows(feat_ref, stream_ref, taps_ref, spec_ref, fwd_ref, inv_ref, out_ref, feat, prod, sums,
            2 * B, blocks)
    middle_ref[...] = prod[0:B, :]

    @pl.when(step == pl.num_programs(0) - 1)
    def _():
        for b in range(blocks):
            sum_ref[b] = put_row_sums(sums[b * B : (b + 1) * B, :], B)


def mr_upper(feat, stream_in, taps, spec, forward, inverse):
    rows, chans = stream_in.shape
    blocks = rows // B - 2
    return pl.pallas_call(
        functools.partial(upper_kernel, blocks=blocks),
        grid=(chans // 256,),
        in_specs=[
            pl.BlockSpec((3, rows, 256), lambda c: (0, 0, c)),
            pl.BlockSpec((rows, 256), lambda c: (0, c)),
            pl.BlockSpec((3, 7, 256), lambda c: (0, 0, c)),
            pl.BlockSpec((2, B, 256), lambda c: (0, 0, c)),
            pl.BlockSpec((2 * B, 2 * B), lambda c: (0, 0)),
            pl.BlockSpec((B, 2 * B), lambda c: (0, 0)),
        ],
        out_specs=[
            pl.BlockSpec((blocks * B, 256), lambda c: (0, c)),
            pl.BlockSpec((blocks, 8, 128), lambda c: (0, 0, 0)),
            pl.BlockSpec((B, 256), lambda c: (0, c)),
        ],
        out_shape=[
            pltpu.HBM((blocks * B, chans), F32),
            jax.ShapeDtypeStruct((blocks, 8, 128), F32),
            pltpu.HBM((B, chans), BF16),
        ],
        scratch_shapes=[
            pltpu.VMEM((3, 2, rows - 120, 128), F32),
            pltpu.VMEM(((blocks + 1) * B, 256), BF16),
            pltpu.VMEM((blocks * B, 128), F32),
        ],
        compiler_params=params(20),
        cost_estimate=cost(2 * 10**9, 14 * 10**6),
        name="mr_upper",
    )(feat, stream_in, taps, spec, forward, inverse)


def lower_kernel(feat_ref, stream_ref, taps_ref, spec_ref, fwd_ref, inv_ref, halo_ref, upper_ref,
                 middle_ref, out_ref, sum_ref, feat, prod, sums, *, blocks):
    step = pl.program_id(0)

    @pl.when(step == 0)
    def _():
        sums[...] = jnp.zeros_like(sums)

    for half in range(2):
        lanes = slice(128 * half, 128 * half + 128)
        for s in range(3):
            feat[s, half, 0:8] = halo_ref[128 + 8 * s : 136 + 8 * s, lanes].astype(F32)
            feat[s, half, 8:] = feat_ref[s, :, lanes].astype(F32)
        before = halo_ref[152:160, lanes].astype(F32) + halo_ref[160:168, lanes].astype(F32)
        sums[2 * B : 2 * B + 8, :] += before * before
    prod[0:B, :] = halo_ref[0:B, :]
    prod[2 * B : 3 * B, :] = middle_ref[...]
    mr_rows(feat_ref, stream_ref, taps_ref, spec_ref, fwd_ref, inv_ref, out_ref, feat, prod, sums,
            0, 2, ready=(0, 2))

    @pl.when(step == pl.num_programs(0) - 1)
    def _():
        for b in range(3):
            sum_ref[b] = put_row_sums(sums[b * B : (b + 1) * B, :], B)
        sum_ref[3:] = upper_ref[...]


def mr_lower(feat, stream_in, taps, spec, forward, inverse, halo, upper, middle):
    rows, chans = stream_in.shape
    blocks = upper.shape[0]
    return pl.pallas_call(
        functools.partial(lower_kernel, blocks=blocks),
        grid=(chans // 256,),
        in_specs=[
            pl.BlockSpec((3, 2 * B, 256), lambda c: (0, 0, c)),
            pl.BlockSpec((2 * B, 256), lambda c: (0, c)),
            pl.BlockSpec((3, 7, 256), lambda c: (0, 0, c)),
            pl.BlockSpec((2, B, 256), lambda c: (0, 0, c)),
            pl.BlockSpec((2 * B, 2 * B), lambda c: (0, 0)),
            pl.BlockSpec((B, 2 * B), lambda c: (0, 0)),
            pl.BlockSpec((168, 256), lambda c: (0, c)),
            pl.BlockSpec((blocks, 8, 128), lambda c: (0, 0, 0)),
            pl.BlockSpec((B, 256), lambda c: (0, c)),
        ],
        out_specs=[
            pl.BlockSpec((2 * B, 256), lambda c: (0, c)),
            pl.BlockSpec((blocks + 3, 8, 128), lambda c: (0, 0, 0)),
        ],
        out_shape=[
            pltpu.HBM((2 * B, chans), F32),
            jax.ShapeDtypeStruct((blocks + 3, 8, 128), F32),
        ],
        scratch_shapes=[
            pltpu.VMEM((3, 2, 2 * B + 8, 128), F32),
            pltpu.VMEM((3 * B, 256), BF16),
            pltpu.VMEM((3 * B, 128), F32),
        ],
        compiler_params=params(14),
        cost_estimate=cost(7 * 10**8, 4 * 10**6),
        name="mr_lower",
    )(feat, stream_in, taps, spec, forward, inverse, halo, upper, *in_hbm(middle))


def state_kernel(low_ref, up_ref, halo_ref, s0_ref, s1_ref, s2_ref, s3_ref, gain_ref, taps_ref,
                 q8_ref, qs_ref, normed_ref, prod_ref, state_ref, copies_ref, inv, rows_f32, *,
                 blocks):
    step = pl.program_id(0)

    @pl.when(step == 0)
    def _():
        total = s0_ref[...] + s1_ref[...] + s2_ref[...] + s3_ref[...]
        scale = lax.rsqrt(total * (1.0 / D) + EPS)
        for b in range(blocks + 1):
            spread = jnp.broadcast_to(scale[b, 0:1, :], (B, B))
            inv[b * B : (b + 1) * B, :] = jnp.transpose(spread)

    for half in range(2):
        lanes = slice(128 * half, 128 * half + 128)
        taps1, taps2 = taps_ref[1, :, lanes], taps_ref[2, :, lanes]
        gain = gain_ref[:, lanes]
        before = halo_ref[0:8, lanes].astype(F32) + halo_ref[8:16, lanes].astype(F32)
        before = (before * inv[2 * B : 2 * B + 8, :] * gain).astype(BF16)
        normed_ref[0:8, lanes] = before
        rows_f32[half, 0:8, :] = before.astype(F32)
        acc = [jnp.zeros((8, 128), F32) for _ in range(MODES)]
        q8 = [jnp.broadcast_to(q8_ref[n : n + 1, lanes], (8, 128)) for n in range(MODES)]
        for b in range(blocks):
            if b < 2:
                x = low_ref[b * B : (b + 1) * B, lanes]
                scale = inv[b * B : (b + 1) * B, :]
            else:
                x = up_ref[(b - 2) * B : (b - 1) * B, lanes]
                scale = inv[(b + 1) * B : (b + 2) * B, :]
            normed = (x * scale * gain).astype(BF16)
            start = 8 + b * B
            normed_ref[start : start + B, lanes] = normed
            rows_f32[half, start : start + B, :] = normed.astype(F32)
            keys = conv7(rows_f32.at[half], taps1, start, B)
            vals = conv7(rows_f32.at[half], taps2, start, B)
            product = (keys * vals).astype(BF16)
            prod_ref[b * B : (b + 1) * B, lanes] = product
            wide = product.astype(F32)
            for i in range(B // 8):
                part = wide[8 * i : 8 * i + 8]
                acc = [a * q + part for a, q in zip(acc, q8)]
            for n in range(MODES):
                state_ref[b, n : n + 1, lanes] = jnp.sum(
                    acc[n] * qs_ref[n, :, lanes], axis=0, keepdims=True
                )
    outgoing = state_ref[blocks - 1].astype(BF16)
    for place in range(copies_ref.shape[0]):
        copies_ref[place] = outgoing


def li_states(low, up, halo, sums, gain, taps, q8, qs, places):
    chans = low.shape[1]
    rows = low.shape[0] + up.shape[0]
    blocks = rows // B
    sum_spec = pl.BlockSpec(sums[0].shape, lambda c: (0, 0, 0))
    return pl.pallas_call(
        functools.partial(state_kernel, blocks=blocks),
        grid=(chans // 256,),
        in_specs=[
            pl.BlockSpec((2 * B, 256), lambda c: (0, c)),
            pl.BlockSpec((rows - 2 * B, 256), lambda c: (0, c)),
            pl.BlockSpec((16, 256), lambda c: (0, c)),
            sum_spec, sum_spec, sum_spec, sum_spec,
            pl.BlockSpec((1, 256), lambda c: (0, c)),
            pl.BlockSpec((3, 7, 256), lambda c: (0, 0, c)),
            pl.BlockSpec((MODES, 256), lambda c: (0, c)),
            pl.BlockSpec((MODES, 8, 256), lambda c: (0, 0, c)),
        ],
        out_specs=[
            pl.BlockSpec((8 + rows, 256), lambda c: (0, c)),
            pl.BlockSpec((rows, 256), lambda c: (0, c)),
            pl.BlockSpec((blocks, MODES, 256), lambda c: (0, 0, c)),
            pl.BlockSpec((places, MODES, 256), lambda c: (0, 0, c)),
        ],
        out_shape=[
            pltpu.HBM((8 + rows, chans), BF16),
            pltpu.HBM((rows, chans), BF16),
            jax.ShapeDtypeStruct((blocks, MODES, chans), F32),
            jax.ShapeDtypeStruct((places, MODES, chans), BF16),
        ],
        scratch_shapes=[
            pltpu.VMEM(((blocks + 1) * B, 128), F32),
            pltpu.VMEM((2, 8 + rows, 128), F32),
        ],
        compiler_params=params(20),
        cost_estimate=cost(90 * 10**6, 9 * 10**6),
        name="li_states",
    )(*in_hbm(low, up), halo, *sums, gain, taps, q8, qs)


def near_kernel(normed_ref, prod_ref, taps_ref, spec_ref, fwd_ref, inv_ref, *rest, blocks):
    near_ref, gate_ref, rows_f32 = rest[-3:]
    forward, inverse = fwd_ref[...], inv_ref[...]
    for half in range(2):
        rows_f32[half] = normed_ref[:, 128 * half : 128 * half + 128].astype(F32)
    for b in range(blocks):
        rows = slice(b * B, (b + 1) * B)
        if b % LI_GROUP == 0:
            windows = [prod_ref[i * B : (i + 1) * B, :] for i in range(b, b + LI_GROUP)]
            found = spectral(windows, forward, spec_ref[0], spec_ref[1], inverse)
        for half in range(2):
            lanes = slice(128 * half, 128 * half + 128)
            gate = conv7(rows_f32.at[half], taps_ref[0, :, lanes], 8 + b * B, B)
            gate_ref[rows, lanes] = gate.astype(BF16)
        near_ref[rows, :] = found[b % LI_GROUP].astype(BF16)


def li_near(normed, product, taps, spec, forward, inverse, part, parts, earlier=()):
    rows, chans = product.shape
    steps = chans // 256 // parts
    at = part * steps
    wide = pl.BlockSpec((rows, 256), lambda c: (0, at + c))
    return pl.pallas_call(
        functools.partial(near_kernel, blocks=rows // B),
        grid=(steps,),
        in_specs=[
            pl.BlockSpec((8 + rows, 256), lambda c: (0, at + c)),
            wide,
            pl.BlockSpec((3, 7, 256), lambda c: (0, 0, at + c)),
            pl.BlockSpec((2, B, 256), lambda c: (0, 0, at + c)),
            pl.BlockSpec((2 * B, B), lambda c: (0, 0)),
            pl.BlockSpec((B, 2 * B), lambda c: (0, 0)),
        ]
        + [pl.BlockSpec(memory_space=pl.ANY)] * len(earlier),
        out_specs=[wide, wide],
        out_shape=[pltpu.HBM((rows, chans), BF16)] * 2,
        scratch_shapes=[pltpu.VMEM((2, 8 + rows, 128), F32)],
        input_output_aliases={6 + i: i for i in range(len(earlier))},
        compiler_params=params(16),
        cost_estimate=cost(10**9 // parts, 8 * 10**6 // parts),
        name="li_near",
    )(*in_hbm(normed, product), taps, spec, forward, inverse, *in_hbm(*earlier))


def far_kernel(low_ref, up_ref, gate_ref, near_ref, state_ref, in_ref, q8_ref, q128_ref, wq_ref,
               out_ref, *, blocks):
    incoming = in_ref[...]
    for b in range(blocks):
        here = incoming if b == 0 else incoming + state_ref[b - 1]
        incoming = incoming * q128_ref[...]
        for half in range(2):
            lanes = slice(128 * half, 128 * half + 128)
            modes = [wq_ref[n, :, lanes] * here[n : n + 1, lanes] for n in range(MODES)]
            for i in range(B // 16):
                total = []
                for part in range(2):
                    level = modes
                    while len(level) > 1:
                        level = [a + c for a, c in zip(level[::2], level[1::2])]
                    total.append(level[0])
                    modes = [
                        m * jnp.broadcast_to(q8_ref[n : n + 1, lanes], (8, 128))
                        for n, m in enumerate(modes)
                    ]
                at = slice(b * B + 16 * i, b * B + 16 * i + 16)
                long = jnp.concatenate(total, axis=0) + near_ref[at, lanes].astype(F32)
                if b < 2:
                    stream = low_ref[at, lanes]
                else:
                    stream = up_ref[(b - 2) * B + 16 * i : (b - 2) * B + 16 * i + 16, lanes]
                gate = gate_ref[at, lanes].astype(F32)
                out_ref[at, lanes] = (stream + gate * long).astype(BF16)


def li_far(low, up, gate, near, states, incoming, q8, q128, wq):
    rows, chans = near.shape
    blocks = rows // B
    wide = pl.BlockSpec((rows, 256), lambda c: (0, c))
    modes = pl.BlockSpec((MODES, 256), lambda c: (0, c))
    return pl.pallas_call(
        functools.partial(far_kernel, blocks=blocks),
        grid=(chans // 256,),
        in_specs=[
            pl.BlockSpec((2 * B, 256), lambda c: (0, c)),
            pl.BlockSpec((rows - 2 * B, 256), lambda c: (0, c)),
            wide,
            wide,
            pl.BlockSpec((blocks, MODES, 256), lambda c: (0, 0, c)),
            modes,
            modes,
            modes,
            pl.BlockSpec((MODES, 8, 256), lambda c: (0, 0, c)),
        ],
        out_specs=wide,
        out_shape=jax.ShapeDtypeStruct((rows, chans), BF16),
        compiler_params=params(16),
        cost_estimate=cost(70 * 10**6, 12 * 10**6),
        name="li_far",
    )(*in_hbm(low, up, gate, near), states, incoming, q8, q128, wq)


def to_next(value):
    lines, places = lax.axis_size("line"), lax.axis_size("place")
    count = lines * places
    return lax.ppermute(value, ("line", "place"), [(i, i + 1) for i in range(count - 1)])


def to_all(value, axis):
    count = lax.axis_size(axis)
    copies = jnp.broadcast_to(value.astype(BF16)[None], (count,) + value.shape)
    return lax.all_to_all(copies, axis, 0, 0)


def weighted(parts, rates, span, upto):
    steps = upto - 1 - jnp.arange(parts.shape[0], dtype=jnp.int32)
    ages = jnp.maximum(steps, 0).astype(F32)[:, None, None] * float(span)
    terms = jnp.exp(-rates[None] * ages) * parts.astype(F32)
    return jnp.sum(jnp.where(steps[:, None, None] >= 0, terms, 0.0), axis=0)


def body(stream_in, features, mr_taps, mr_filter, norm_gain, li_taps, modal_rates, modal_weights):
    rows = stream_in.shape[0]
    feat, stream_in = in_hbm(jnp.transpose(features, (1, 0, 2)), stream_in)
    mr_t = jnp.transpose(mr_taps, (0, 2, 1))
    li_t = jnp.transpose(li_taps, (0, 2, 1))
    rates = jnp.transpose(modal_rates)
    weights = jnp.transpose(modal_weights)
    gain = norm_gain[None, :]
    fwd_np, inv_np = dft_tables()
    forward = jnp.asarray(fwd_np, BF16)
    inverse = jnp.asarray(inv_np, BF16)
    half_fwd = jnp.asarray(fwd_np[:, :B], F32)

    near_high = fwd_np[:, :B].astype(BF16)
    near_low = (fwd_np[:, :B] - near_high.astype(np.float64)).astype(BF16)
    split_fwd = jnp.asarray(np.concatenate([near_high, near_low], axis=1))
    bundle, mr_spec = mr_tail(feat, stream_in, mr_t, mr_filter, split_fwd)
    halo = to_next(bundle)
    up, up_sums, middle = mr_upper(feat, stream_in, mr_t, mr_spec, forward, inverse[B:])
    low, own = mr_lower(feat, stream_in, mr_t, mr_spec, forward, inverse[B:], halo, up_sums, middle)
    ways = lax.axis_size("tp")
    sums = [own] + [
        lax.ppermute(own, "tp", [(i, (i + k) % ways) for i in range(ways)]) for k in range(1, ways)
    ]

    rates, weights, own = lax.optimization_barrier((rates, weights, own))
    scaled = weights * jnp.sqrt(1.0 - jnp.exp(-2.0 * rates))
    lags = jnp.arange(B, dtype=F32)
    coarse = jnp.exp(-rates[None] * (8.0 * lags)[: B // 8, None, None])
    fine = scaled[:, None] * jnp.exp(-rates[:, None] * lags[None, :8, None])
    coarse, fine = lax.optimization_barrier((coarse, fine))
    near_taps = jnp.sum(coarse[:, :, None] * fine[None], axis=1).reshape(B, -1)
    li_spec = jnp.dot(half_fwd, near_taps, precision=lax.Precision.HIGH).reshape(2, B, -1)
    within = jnp.arange(8, dtype=F32)[None, :, None]
    q8 = jnp.exp(-8.0 * rates)
    q128 = jnp.exp(-float(B) * rates)
    qs = jnp.exp(-rates[:, None, :] * (7.0 - within))
    wq = scaled[:, None, :] * jnp.exp(-rates[:, None, :] * (within + 1.0))
    gain, li_spec, wq, q128 = lax.optimization_barrier((gain, li_spec, wq, q128))

    near_args = (li_t, li_spec, forward[:, :B], inverse[:B])
    place, line = lax.axis_index("place"), lax.axis_index("line")
    places = lax.axis_size("place")
    normed, product, states, copies = li_states(
        low, up, halo[152:168], sums, gain, li_t, q8, qs, places
    )
    with jax.named_scope("scan_places"):
        parts = lax.all_to_all(copies, "place", 0, 0)
    first = li_near(normed, product, *near_args, 0, 2)
    with jax.named_scope("scan_places"):
        parts, first = lax.optimization_barrier((parts, first))
        whole = weighted(parts, rates, rows, places)
        prefix = weighted(parts, rates, rows, place)
    with jax.named_scope("scan_lines"):
        parts = to_all(whole, "line")
    normed, whole = lax.optimization_barrier((normed, whole))
    near, gate = li_near(normed, product, *near_args, 1, 2, first)
    with jax.named_scope("scan_lines"):
        parts, near, gate = lax.optimization_barrier((parts, near, gate))
        before = weighted(parts, rates, rows * places, line)
        incoming = prefix + before * jnp.exp(-rates * (rows * place.astype(F32)))
    return li_far(low, up, gate, near, states, incoming, q8, q128, wq)


def solution(mesh):
    ctx, tp = mesh.devices.shape
    places = 8 if ctx % 8 == 0 else ctx
    split = jax.sharding.Mesh(
        mesh.devices.reshape(ctx // places, places, tp), ("line", "place", "tp")
    )
    seq = ("line", "place")
    in_specs = (
        P(seq, "tp"),
        P(seq, None, "tp"),
        P(None, "tp", None),
        P("tp", None),
        P("tp"),
        P(None, "tp", None),
        P("tp", None),
        P("tp", None),
    )
    return jax.shard_map(
        body, mesh=split, in_specs=in_specs, out_specs=P(seq, "tp"), check_vma=False
    )
```
